32 devices in a mesh: parts: 2 (over y), slab: 4 (over z), blk: 2 (over x), head: 2 (over core).
Axes of the slice: x: 2, y: 2, z: 4, core: 2. Of those that a mesh axis runs over, the one named last changes fastest.
Arguments:
- features: bfloat16 [4096, 512], P(('parts', 'slab', 'blk')), parts along dimension 0, may hold values from -16 to 16
- cotangent: bfloat16 [4096, 512], P(('parts', 'slab', 'blk')), parts along dimension 0, may hold values from -6 to 6
- w_query: bfloat16 [512, 512], P(None, 'head'), may hold values from -0.25 to 0.25
- w_key: bfloat16 [512, 512], P(None, 'head'), may hold values from -0.25 to 0.25
- w_value: bfloat16 [512, 512], P(None, 'head'), may hold values from -0.25 to 0.25
- w_out: bfloat16 [512, 512], P('head'), may hold values from -0.25 to 0.25
- adjacency: int32 [32, 3], P(('parts', 'slab', 'blk')), parts along dimension 0, may hold values from 0 to 1, as said below
- partner: int32 [3, 32], P(None, ('parts', 'slab', 'blk')), parts along dimension 1, may hold values from 0 to 15, as said below
- node_order: int32 [4096], P(('parts', 'slab', 'blk')), parts along dimension 0, may hold values from 0 to 255, as said below
Outputs:
- grad_input: bfloat16 [4096, 512], P(('parts', 'slab', 'blk'), 'head'), parts along dimension 0
The draws below stay inside these ranges and needn't reach their ends.
There are 2 independent parts, one for each index of `parts`. The reference program is written for one: setup_inputs(seed, part) draws one part's arguments, and reference() takes and returns one part's arrays. A program takes and returns all parts, laid end to end along the dimension named above; an argument that names none is the same for every part. Nothing has to cross between parts.
Inputs may be any that keep to these rules, and one draw needn't show every extreme that they name: `adjacency`: column 1 (the block itself) is always 1. partner[m, g] is the block at the same position among its device's 2 blocks, on the device of the same blk index in another slab; partner[m, partner[m, g]] = g. Of the 3 * 2 (matching, block) pairs of one device, at most 2 have their partner in one slab, and on every device exactly 2 do for some slab. `node_order`: within each device's 2 * 128 positions, a permutation of the device's rows.
All inputs are finite; a program needn't handle non-finite values.
Results may differ from the reference program's by a relative error of at most 0.013.
The reference program's roundings to bfloat16 on the way count: a program that leaves them out, or rounds other values in their place, can miss the bound.
Values may be sent and summed in bfloat16 or wider, within the bound.
A program may use at most 64 MiB of HBM per device.

```python
import jax
import jax.numpy as jnp
from jax import lax

D = 512
HEADS = 8
BLOCK = 128
BPD = 2
HEAD_DIM = 64
TOTAL_BLOCKS = 16
NODES = 2048
CAP = 2
N_SLAB = 4
N_BLK = 2


def draw_features(key, part):
    return jnp.clip(jax.random.normal(key, (NODES, D), jnp.float32), -6.0, 6.0).astype(jnp.bfloat16)


def draw_adjacency(key, part):
    bits = jax.random.randint(jax.random.fold_in(key, 7), (TOTAL_BLOCKS, 3), 0, 2, dtype=jnp.int32)
    return bits.at[:, 1].set(1)


def draw_node_order(key, part):
    device_count = NODES // (BPD * BLOCK)
    device_keys = jax.random.split(jax.random.fold_in(key, 5), device_count)
    orders = jax.vmap(lambda one_key: jax.random.permutation(one_key, BPD * BLOCK))(device_keys)
    return orders.reshape(NODES).astype(jnp.int32)


def draw_partner(key, part):
    item_count = 3 * BPD

    def column_codes(column_key):
        codes = jax.random.permutation(column_key, N_SLAB - 1).astype(jnp.int32) + 1
        repeated = jnp.repeat(codes, CAP, total_repeat_length=(N_SLAB - 1) * CAP)[:item_count]
        shuffle = jax.random.permutation(jax.random.fold_in(column_key, 1), item_count)
        return repeated[shuffle]
    codes = jax.vmap(column_codes)(jax.random.split(jax.random.fold_in(key, 11), N_BLK))
    codes = jnp.transpose(codes.reshape(N_BLK, 3, BPD), (1, 0, 2))
    label_keys = jax.random.split(jax.random.fold_in(key, 12), N_BLK)
    labels = jax.vmap(lambda one_key: jax.random.permutation(one_key, N_SLAB))(label_keys)
    labels = labels.astype(jnp.int32).reshape(N_BLK, N_SLAB)
    unlabel = jnp.argsort(labels, axis=-1).astype(jnp.int32)
    unlabel = jnp.broadcast_to(unlabel[None], (3, N_BLK, N_SLAB))
    target = jnp.bitwise_xor(labels[None, :, :, None], codes[:, :, None, :])
    slab_of = jnp.take_along_axis(unlabel, target.reshape(3, N_BLK, N_SLAB * BPD), axis=2)
    slab_of = slab_of.reshape(3, N_BLK, N_SLAB, BPD)
    column = jnp.arange(N_BLK, dtype=jnp.int32)[None, :, None, None]
    position = jnp.arange(BPD, dtype=jnp.int32)[None, None, None, :]
    global_id = (slab_of * N_BLK + column) * BPD + position
    return jnp.transpose(global_id, (0, 2, 1, 3)).reshape(3, TOTAL_BLOCKS).astype(jnp.int32)


def shard_levels(rng, shape, cuts, low, largest):
    def one(dim, parts):
        steps = jax.random.uniform(jax.random.fold_in(jax.random.fold_in(rng, 6), dim), (parts,), jnp.float32, low / len(cuts), largest / len(cuts))
        return jnp.repeat(jnp.exp(steps), shape[dim] // parts).reshape((-1,) + (1,) * (len(shape) - dim - 1))

    gain = one(*cuts[0])
    for cut in cuts[1:]:
        gain = gain * one(*cut)
    return gain


def scatter_about(stream_key, dims, width, most, cuts=(), held_as=jnp.bfloat16):
    level = shard_levels(stream_key, dims, cuts, -0.22, 0.18) if cuts else 1.0
    values = jax.random.normal(stream_key, dims, jnp.float32) * width * level
    return jnp.minimum(jnp.maximum(values, -most), most).astype(held_as)


def setup_inputs(seed: int = 0, part: int = 0) -> dict:
    streams_of = jax.random.split(jax.random.key(seed), 10)
    own_keys = jax.random.split(jax.random.fold_in(streams_of[9], part), 10)
    features = draw_features(jax.random.fold_in(jax.random.fold_in(streams_of[9], part), 71), part)
    cotangent = scatter_about(own_keys[1], (NODES, D), 1.0, 6.0, ((0, 8),))
    w_query = scatter_about(streams_of[2], (D, D), D ** -0.5, 0.25, ((1, 2),))
    w_key = scatter_about(streams_of[3], (D, D), D ** -0.5, 0.25, ((1, 2),))
    w_value = scatter_about(streams_of[4], (D, D), D ** -0.5, 0.25, ((1, 2),))
    w_out = scatter_about(streams_of[5], (D, D), D ** -0.5, 0.25, ((0, 2),))
    adjacency = draw_adjacency(jax.random.fold_in(jax.random.fold_in(streams_of[9], part), 71), part)
    partner = draw_partner(jax.random.fold_in(jax.random.fold_in(streams_of[9], part), 71), part)
    node_order = draw_node_order(jax.random.fold_in(jax.random.fold_in(streams_of[9], part), 71), part)
    return dict(features=features, cotangent=cotangent, w_query=w_query, w_key=w_key, w_value=w_value, w_out=w_out, adjacency=adjacency, partner=partner, node_order=node_order)


def reference(features, cotangent, w_query, w_key, w_value, w_out, adjacency, partner, node_order):
    device_rows = BPD * BLOCK
    cycle_len = N_BLK * BPD
    score_scale = HEAD_DIM ** -0.5
    source_rows = (jnp.arange(NODES, dtype=jnp.int32) // device_rows) * device_rows + node_order.astype(jnp.int32)
    blocked_input = features[source_rows]
    blocked_grad = cotangent[source_rows]
    query_rows = jnp.dot(blocked_input, w_query, preferred_element_type=jnp.float32).astype(jnp.bfloat16)
    key_rows = jnp.dot(blocked_input, w_key, preferred_element_type=jnp.float32).astype(jnp.bfloat16)
    value_rows = jnp.dot(blocked_input, w_value, preferred_element_type=jnp.float32).astype(jnp.bfloat16)
    grad_mix = jnp.dot(blocked_grad, jnp.transpose(w_out), preferred_element_type=jnp.float32).astype(jnp.bfloat16)
    block_shape = (TOTAL_BLOCKS, BLOCK, HEADS, HEAD_DIM)
    key_blocks = key_rows.reshape(block_shape)
    value_blocks = value_rows.reshape(block_shape)
    block_ids = jnp.arange(TOTAL_BLOCKS, dtype=jnp.int32)
    slab_base = (block_ids // cycle_len) * cycle_len
    offsets = jnp.arange(3, dtype=jnp.int32) - 1
    near_ids = slab_base[:, None] + (block_ids[:, None] % cycle_len + offsets[None, :]) % cycle_len
    chosen = jnp.concatenate([near_ids, jnp.transpose(partner).astype(jnp.int32)], axis=1)
    switch = jnp.concatenate([adjacency > 0, jnp.ones((TOTAL_BLOCKS, 3), dtype=bool)], axis=1)
    groups = TOTAL_BLOCKS // BPD

    def grouped(source):
        return source.reshape((groups, BPD) + source.shape[1:])

    def visit(totals, pieces):
        grad_keys, grad_values = totals
        queries, upstream, picked, wanted = pieces
        queries = queries.astype(jnp.float32)
        upstream = upstream.astype(jnp.float32)
        keys_here = key_blocks[picked].reshape(BPD, 6 * BLOCK, HEADS, HEAD_DIM).astype(jnp.float32)
        values_here = value_blocks[picked].reshape(BPD, 6 * BLOCK, HEADS, HEAD_DIM).astype(jnp.float32)
        scores = jnp.einsum('gqhd,gkhd->ghqk', queries, keys_here) * score_scale
        keys_on = jnp.repeat(wanted, BLOCK, axis=1)
        scores = jnp.where(keys_on[:, None, None, :], scores, -jnp.inf)
        row_peak = jnp.max(scores, axis=-1, keepdims=True)
        row_total = jnp.log(jnp.sum(jnp.exp(scores - row_peak), axis=-1, keepdims=True)) + row_peak
        attention = jnp.exp(scores - row_total)
        attention_low = lax.optimization_barrier(attention.astype(jnp.bfloat16)).astype(jnp.float32)
        mixed_rows = jnp.einsum('ghqk,gkhd->gqhd', attention_low, values_here)
        row_dot = jnp.transpose(jnp.sum(upstream * mixed_rows, axis=-1), (0, 2, 1))
        grad_attention = jnp.einsum('gqhd,gkhd->ghqk', upstream, values_here)
        grad_scores = attention * (grad_attention - row_dot[..., None])
        grad_scores = lax.optimization_barrier(grad_scores.astype(jnp.bfloat16)).astype(jnp.float32)
        grad_query = score_scale * jnp.einsum('ghqk,gkhd->gqhd', grad_scores, keys_here)
        key_terms = score_scale * jnp.einsum('ghqk,gqhd->gkhd', grad_scores, queries)
        value_terms = jnp.einsum('ghqk,gqhd->gkhd', attention_low, upstream)
        flat_ids = picked.reshape(-1)
        grad_keys = grad_keys.at[flat_ids].add(key_terms.reshape(BPD * 6, BLOCK, HEADS, HEAD_DIM))
        grad_values = grad_values.at[flat_ids].add(value_terms.reshape(BPD * 6, BLOCK, HEADS, HEAD_DIM))
        return (grad_keys, grad_values), grad_query

    start = (jnp.zeros(block_shape, jnp.float32), jnp.zeros(block_shape, jnp.float32))
    pieces = (grouped(query_rows.reshape(block_shape)), grouped(grad_mix.reshape(block_shape)), grouped(chosen), grouped(switch))
    (grad_keys, grad_values), grad_queries = lax.scan(visit, start, pieces)
    grad_query = grad_queries.reshape(NODES, D).astype(jnp.bfloat16)
    grad_key = grad_keys.reshape(NODES, D).astype(jnp.bfloat16)
    grad_value = grad_values.reshape(NODES, D).astype(jnp.bfloat16)
    branch = jnp.dot(grad_query, jnp.transpose(w_query), preferred_element_type=jnp.float32)
    branch = branch + jnp.dot(grad_key, jnp.transpose(w_key), preferred_element_type=jnp.float32)
    branch = branch + jnp.dot(grad_value, jnp.transpose(w_value), preferred_element_type=jnp.float32)
    grad_input = jnp.zeros((NODES, D), jnp.float32).at[source_rows].set(branch)
    return grad_input.astype(jnp.bfloat16)
```

```python
import functools

import jax
import jax.numpy as jnp
from jax import lax
from jax.experimental import pallas as pl
from jax.experimental.pallas import tpu as pltpu
from jax.sharding import PartitionSpec as P

HEAD_DIM = 64
OFF = -1e30
NT = (((1,), (1,)), ((), ()))
TN = (((0,), (0,)), ((), ()))
F32, BF16 = jnp.float32, jnp.bfloat16
MESH = pl.DeviceIdType.MESH


def mm(a, b):
    return jnp.dot(a, b, preferred_element_type=F32)


def mm_nt(a, b):
    return lax.dot_general(a, b, NT, preferred_element_type=F32)


def kernel(
    n, nb,
    feat_hbm, cot_hbm, w_q_hbm, w_k_hbm, w_v_hbm, w_o_hbm, adj_hbm, part_hbm, order_hbm, out,
    feat, cot, w_q, w_k, w_v, w_o, adj, part, order, fetch,
    perm, own_x, own_c, rx, rc, k_own, v_own, kt_all, qm_own, gm_own,
    qm_far, e_loc, g_loc, e_far, g_far, s_back, ds_all, rows_loc, rows_far,
    stat, stat_near_own, stat_far, near_far,
    dq, dk, dv, give, take,
    x_send, x_recv, xf_send, xf_recv, c_send, c_recv, cf_send, cf_recv,
    t_send, t_recv, h_send, h_recv, hop_send, part_out, acks,
):
    rows, width = feat.shape
    half = width // 2
    cols = w_q.shape[1]
    heads = cols // HEAD_DIM
    block = rows // 2
    lanes = heads * block
    scale = HEAD_DIM ** -0.5
    h, slab, x = (lax.axis_index(a) for a in ("head", "slab", "blk"))
    behind, ahead = {"blk": lax.rem(x + nb - 1, nb)}, {"blk": lax.rem(x + 1, nb)}
    twin = {"head": 1 - h}

    def onward(d):
        return {"slab": lax.rem(slab + d, n)}

    line = n == 4 and nb == 2
    at_start, at_end = slab == 0, slab == n - 1
    inner = jnp.logical_and(slab > 0, slab < n - 1)

    def each(f):
        if n <= 4:
            for d in range(1, n):
                f(d)
        else:
            lax.fori_loop(1, n, lambda d, c: (f(d), c)[1], 0)

    def slots(f):
        f(0)
        each(f)

    def each_direct(f):
        if line:
            f(2)
            pl.when(jnp.logical_not(at_end))(lambda: f(1))
            pl.when(jnp.logical_not(at_start))(lambda: f(3))
        else:
            each(f)

    loads = [
        pltpu.make_async_copy(src, dst, fetch.at[i])
        for i, (src, dst) in enumerate((
            (order_hbm, order), (feat_hbm, feat), (cot_hbm, cot), (w_q_hbm, w_q), (w_k_hbm, w_k),
            (w_v_hbm, w_v), (w_o_hbm, w_o), (adj_hbm, adj), (part_hbm, part),
        ))
    ]
    for load in loads:
        load.start()
    barrier = pltpu.get_barrier_semaphore()

    def greet(where):
        pl.semaphore_signal(barrier, inc=1, device_id=where, device_id_type=MESH)

    def ack(where, k):
        pl.semaphore_signal(acks.at[k], inc=1, device_id=where, device_id_type=MESH)

    BLK, TWIN = 0, n

    if line:
        pl.when(h == 0)(lambda: greet(twin))
        pl.when(x == 0)(lambda: greet(ahead))
        for d in range(1, n):
            pl.when(slab + d < n)(lambda d=d: greet({"slab": slab + d}))
    else:
        greet(behind)
        greet(ahead)
        greet(twin)
        each(lambda d: greet(onward(d)))

    def enter():
        if line:
            earlier = slab + x + h
            pl.when(earlier > 0)(lambda: pl.semaphore_wait(barrier, earlier))
            for d in range(1, n):
                pl.when(slab >= d)(lambda d=d: ack({"slab": slab - d}, d))
            pl.when(x == 1)(lambda: ack(behind, BLK))
            pl.when(h == 1)(lambda: ack(twin, TWIN))
        else:
            pl.semaphore_wait(barrier, n + 2)

    def answered(k):
        pl.semaphore_wait(acks.at[k], 1)

    def copy(src, dst, send, recv, where):
        return pltpu.make_async_remote_copy(
            src_ref=src, dst_ref=dst, send_sem=send, recv_sem=recv,
            device_id=where, device_id_type=MESH,
        )

    low, high = pl.ds(0, block), pl.ds(block, block)

    def near_copies(own, far, send, recv):
        return (
            copy(own.at[h, low], far.at[0, h, high], send.at[n], recv.at[n], behind),
            copy(own.at[h, high], far.at[0, h, low], send.at[0], recv.at[0], ahead),
        )

    def slab_copy(own, far, send, recv, d):
        return copy(own.at[h], far.at[d, h], send.at[d], recv.at[d], onward(d))

    def twin_copy(far, send, recv, i):
        return copy(far.at[i, h], far.at[i, h], send.at[i], recv.at[i], twin)

    x_near = functools.partial(near_copies, own_x, rx, x_send, x_recv)
    c_near = functools.partial(near_copies, own_c, rc, c_send, c_recv)
    x_slab = functools.partial(slab_copy, own_x, rx, x_send, x_recv)
    c_slab = functools.partial(slab_copy, own_c, rc, c_send, c_recv)
    x_twin = functools.partial(twin_copy, rx, xf_send, xf_recv)
    c_twin = functools.partial(twin_copy, rc, cf_send, cf_recv)

    def hop_copy(far, recv, k):
        up = slab == n - 2
        slot = jnp.where(up, 3, 1)
        return copy(
            far.at[2, h], far.at[slot, h], hop_send.at[k], recv.at[slot],
            {"slab": jnp.where(up, n - 1, 0)},
        )

    x_hop = functools.partial(hop_copy, rx, x_recv, 0)
    c_hop = functools.partial(hop_copy, rc, c_recv, 1)

    def stat_near():
        return (
            copy(stat_near_own.at[0], near_far.at[1], t_send.at[n], t_recv.at[n], behind),
            copy(stat_near_own.at[1], near_far.at[0], t_send.at[0], t_recv.at[0], ahead),
        )

    def stat_slab(d):
        return copy(stat, stat_far.at[d], t_send.at[d], t_recv.at[d], onward(d))

    def send_slab(copy_of, plan, wait=False):
        for z, ds in plan.items():
            @pl.when(slab == z)
            def _(z=z, ds=ds):
                for d in ds:
                    if wait and z + d < n:
                        answered(d)
                    copy_of(d).start()

    loads[0].wait()
    loads[1].wait()
    hot = lax.broadcasted_iota(jnp.int32, (rows, rows), 0) == order[...]
    perm[...] = jnp.where(hot, 1.0, 0.0).astype(BF16)
    x_all = lax.dot_general(perm[...], feat[...], TN, preferred_element_type=F32).astype(BF16)
    own_x[0] = x_all[:, :half]
    own_x[1] = x_all[:, half:]

    enter()
    if line:
        send_slab(x_slab, {0: (1, 2), 1: (3, 1, 2), 2: (2, 3, 1), 3: (2, 3)}, wait=True)
        pl.when(x == 0)(lambda: answered(BLK))
        for c in x_near():
            c.start()
    else:
        for c in x_near():
            c.start()
        each_direct(lambda d: x_slab(d).start())

    loads[2].wait()
    c_all = lax.dot_general(perm[...], cot[...], TN, preferred_element_type=F32).astype(BF16)
    own_c[0] = c_all[:, :half]
    own_c[1] = c_all[:, half:]
    for c in c_near():
        c.start()
    if line:
        send_slab(c_slab, {0: (1, 2), 1: (3,), 2: (2, 3, 1), 3: (2, 3)})
    else:
        each_direct(lambda d: c_slab(d).start())

    for load in loads[3:]:
        load.wait()

    lane_head = lax.broadcasted_iota(jnp.int32, (1, cols), 1) // HEAD_DIM
    masks = [jnp.where(lane_head == i, 1.0, 0.0).astype(BF16) for i in range(heads)]

    def masked(value, b):
        part_rows = value[b * block:(b + 1) * block]
        return jnp.concatenate([part_rows * mask for mask in masks], axis=0)

    def weight_flag(flag):
        return jnp.where(flag > 0, 1.0, 0.0).astype(F32)

    def far_weight(i, b):
        if isinstance(i, int) and i == 0:
            return weight_flag(adj[0, 0] if b == 0 else adj[1, 2])
        source = lax.rem(slab + n - i, n)
        total = jnp.float32(0.0)
        for m in range(3):
            total = total + jnp.where(lax.div(part[b, m], 2 * nb) == source, 1.0, 0.0)
        return total

    def local_weight(kb, qb):
        if kb == qb:
            return jnp.float32(1.0)
        return weight_flag(adj[0, 2] if qb == 0 else adj[1, 0])

    def bias(w):
        return jnp.where(w > 0.0, 0.0, OFF).astype(F32)

    def key_cols(i):
        if isinstance(i, int):
            return pl.ds((2 + i) * block, block)
        return pl.ds(pl.multiple_of((2 + i) * block, block), block)

    q_all = (mm(x_all, w_q[...]).astype(BF16) * scale).astype(BF16)
    k_all = mm(x_all, w_k[...])
    k_own[...] = k_all.astype(BF16)
    kt = k_all.T.astype(BF16)
    for b in range(2):
        kt_all[b, :, 0:2 * block] = kt
    v_own[...] = mm(x_all, w_v[...]).astype(BF16)
    g_all = mm_nt(c_all, w_o[...]).astype(BF16)
    for b in range(2):
        qm_own[b] = masked(q_all, b)
        gm_own[b] = masked(g_all, b)

    for b in range(2):
        s = mm_nt(k_own[...], qm_own[b])
        g = mm_nt(v_own[...], gm_own[b])
        parts = [s[kb * block:(kb + 1) * block] + bias(local_weight(kb, b)) for kb in range(2)]
        top = jnp.maximum(
            jnp.max(parts[0], axis=0, keepdims=True), jnp.max(parts[1], axis=0, keepdims=True)
        )
        e = jnp.exp(jnp.concatenate(parts, axis=0) - top)
        e_loc[b] = e
        g_loc[b] = g
        rows_loc[b, 0:1] = top
        rows_loc[b, 1:2] = jnp.sum(e, axis=0, keepdims=True)
        rows_loc[b, 2:3] = jnp.sum(e * g, axis=0, keepdims=True)

    def forward_slot(i):
        x0, x1 = rx[i, 0], rx[i, 1]

        def project(w):
            return mm(x0, w[:half, :]) + mm(x1, w[half:, :])

        q = (project(w_q).astype(BF16) * scale).astype(BF16)
        k32 = project(w_k)
        k = k32.astype(BF16)
        kt = k32.T.astype(BF16)
        v = project(w_v).astype(BF16)
        for b in range(2):
            here = slice(b * block, (b + 1) * block)
            kt_all[b, :, key_cols(i)] = kt[:, here]
            qm = masked(q, b)
            qm_far[i, b] = qm
            s = mm_nt(k[here], qm_own[b])
            g = mm_nt(v[here], gm_own[b])
            top = jnp.max(s, axis=0, keepdims=True)
            e = jnp.exp(s - top)
            e_far[i, b] = e
            g_far[i, b] = g
            rows_far[i, b, 0:1] = top
            rows_far[i, b, 1:2] = jnp.sum(e, axis=0, keepdims=True)
            rows_far[i, b, 2:3] = jnp.sum(e * g, axis=0, keepdims=True)
            s_back[i, b] = mm_nt(k_own[here, :], qm)

    first, last = (jnp.where(at_start, 3, 1), jnp.where(at_start, 1, 3)) if line else (None, None)

    def arrive(slab_copy_of, twin_of, hop, d):
        slab_copy_of(d).wait_recv()
        if hop is not None:
            @pl.when(inner)
            def _():
                hop().start()
        twin_of(d).start()

    def near_arrive(near, twin_of):
        for c in near():
            c.wait_recv()
        twin_of(0).start()

    if line:
        pl.when(h == 0)(lambda: answered(TWIN))
    near_arrive(x_near, x_twin)
    if line:
        arrive(x_slab, x_twin, None, first)
        x_twin(0).wait_recv()
        forward_slot(0)
        arrive(x_slab, x_twin, x_hop, 2)
        send_slab(c_slab, {1: (1, 2)})
        x_twin(first).wait_recv()
        forward_slot(first)
        x_twin(2).wait_recv()
        forward_slot(2)
        arrive(x_slab, x_twin, None, last)
        x_twin(last).wait_recv()
        forward_slot(last)
    else:
        x_twin(0).wait_recv()
        forward_slot(0)

        def step(d):
            arrive(x_slab, x_twin, None, d)
            x_twin(d).wait_recv()
            forward_slot(d)

        each(step)

    def pack(ref, at, top, dot):
        for j in range(lanes // 128):
            part_cols = slice(j * 128, (j + 1) * 128)
            ref[at, j:j + 1, :] = top[:, part_cols]
            ref[at, 4 + j:5 + j, :] = dot[:, part_cols]

    def unpack(tile):
        count = lanes // 128
        return (
            jnp.concatenate([tile[j:j + 1, :] for j in range(count)], axis=1),
            jnp.concatenate([tile[4 + j:5 + j, :] for j in range(count)], axis=1),
        )

    for b in range(2):
        rows_loc[b, 3:4] = rows_loc[b, 0:1]

        def far_top(i):
            rows_loc[b, 3:4] = jnp.maximum(
                rows_loc[b, 3:4], rows_far[i, b, 0:1] + bias(far_weight(i, b))
            )

        slots(far_top)
        top = rows_loc[b, 3:4]
        share_loc = jnp.exp(rows_loc[b, 0:1] - top)
        rows_loc[b, 4:5] = rows_loc[b, 1:2] * share_loc
        rows_loc[b, 5:6] = rows_loc[b, 2:3] * share_loc

        def far_sum(i):
            w = far_weight(i, b)
            f = w * jnp.exp(rows_far[i, b, 0:1] + (bias(w) - top))
            rows_far[i, b, 3:4] = f
            rows_loc[b, 4:5] += f * rows_far[i, b, 1:2]
            rows_loc[b, 5:6] += f * rows_far[i, b, 2:3]

        slots(far_sum)
        inverse = 1.0 / rows_loc[b, 4:5]
        dot = rows_loc[b, 5:6] * inverse
        row_total = top + jnp.log(rows_loc[b, 4:5])
        rows_loc[b, 3:4] = share_loc * inverse
        rows_loc[b, 4:5] = inverse
        rows_loc[b, 5:6] = dot
        pack(stat, b, row_total, dot)
        flag = weight_flag(adj[0, 0] if b == 0 else adj[1, 2])
        pack(stat_near_own, b, jnp.where(flag > 0.0, row_total, -OFF), dot)

    if line:
        pl.when(at_start)(lambda: answered(3))
    each(lambda d: stat_slab(d).start())
    for c in stat_near():
        c.start()

    near_arrive(c_near, c_twin)
    if line:
        arrive(c_slab, c_twin, None, first)
        arrive(c_slab, c_twin, c_hop, 2)

    for b in range(2):
        qcols = slice(b * block, (b + 1) * block)
        dot = rows_loc[b, 5:6]
        p = e_loc[b] * rows_loc[b, 3:4]
        ds = (p * (g_loc[b] - dot)).astype(BF16)
        p_low = p.astype(BF16)
        ds_all[b, 0:2 * block] = ds
        if b == 0:
            dv[...] = mm(p_low, gm_own[b])
            dk[...] = mm(ds, qm_own[b])
        else:
            dv[...] += mm(p_low, gm_own[b])
            dk[...] += mm(ds, qm_own[b])

        def query_grad(i):
            f = rows_far[i, b, 3:4] * rows_loc[b, 4:5]
            ds_all[b, key_cols(i)] = (
                e_far[i, b] * f * (g_far[i, b] - rows_loc[b, 5:6])
            ).astype(BF16)

        slots(query_grad)
        for j in range(heads):
            hd = slice(j * HEAD_DIM, (j + 1) * HEAD_DIM)
            dq[hd, qcols] = mm(kt_all[b, hd, :], ds_all[b, :, j * block:(j + 1) * block])

    dq_low = (dq[...].T * scale).astype(BF16)

    def half_at(which):
        return pl.ds(pl.multiple_of(which * half, half), half)

    for k, which in enumerate((1 - h, h)):
        part_out[k] = mm_nt(dq_low, w_q[half_at(which), :])

    def backward_slot(i):
        c0, c1 = rc[i, 0], rc[i, 1]
        g = (mm_nt(c0, w_o[:, :half]) + mm_nt(c1, w_o[:, half:])).astype(BF16)
        for b in range(2):
            here = slice(b * block, (b + 1) * block)
            gm = masked(g, b)
            if isinstance(i, int) and i == 0:
                row_total, dot = unpack(near_far[b])
                w = jnp.float32(1.0)
            else:
                row_total, dot = unpack(stat_far[i, b])
                w = far_weight(i, b)
                row_total = jnp.where(w > 0.0, row_total, -OFF)
            p = jnp.exp(s_back[i, b] - row_total) * w
            gp = mm_nt(v_own[here, :], gm)
            ds = (p * (gp - dot)).astype(BF16)
            dv[here, :] += mm(p.astype(BF16), gm)
            dk[here, :] += mm(ds, qm_far[i, b])

    for c in stat_near():
        c.wait_recv()
    c_twin(0).wait_recv()
    backward_slot(0)
    if line:
        for i in (first, 2):
            stat_slab(i).wait_recv()
            c_twin(i).wait_recv()
            backward_slot(i)
        arrive(c_slab, c_twin, None, last)
        stat_slab(last).wait_recv()
        c_twin(last).wait_recv()
        backward_slot(last)
    else:
        def back_step(d):
            arrive(c_slab, c_twin, None, d)
            stat_slab(d).wait_recv()
            c_twin(d).wait_recv()
            backward_slot(d)

        each(back_step)

    dk_low, dv_low = dk[...].astype(BF16), dv[...].astype(BF16)

    def share(k, which):
        at = half_at(which)
        return part_out[k] + mm_nt(dk_low, w_k[at, :]) + mm_nt(dv_low, w_v[at, :])

    give[...] = share(0, 1 - h).astype(BF16)
    swap = copy(give, take, h_send, h_recv, twin)
    swap.start()
    mine = share(1, h)
    swap.wait_recv()
    branch = (mine + take[...].astype(F32)).astype(BF16)
    out[...] = mm(perm[...], branch).astype(BF16)

    swap.wait_send()
    for c in (*x_near(), *c_near(), *stat_near(), x_twin(0), c_twin(0)):
        c.wait_send()

    def finish(d):
        for c in (stat_slab(d), x_twin(d), c_twin(d)):
            c.wait_send()

    each(finish)
    each_direct(lambda d: x_slab(d).wait_send())
    each_direct(lambda d: c_slab(d).wait_send())
    if line:
        @pl.when(inner)
        def _():
            x_hop().wait_send()
            c_hop().wait_send()


def body(features, cotangent, w_query, w_key, w_value, w_out, adjacency, partner, node_order):
    n, nb = lax.axis_size("slab"), lax.axis_size("blk")
    rows, width = features.shape
    cols = w_query.shape[1]
    half, block = width // 2, rows // 2
    lanes = (cols // HEAD_DIM) * block
    keys = (n + 2) * block
    vm, dma = pltpu.VMEM, pltpu.SemaphoreType.DMA
    vmem, hbm = (pl.BlockSpec(memory_space=m) for m in (pltpu.VMEM, pltpu.HBM))
    return pl.pallas_call(
        functools.partial(kernel, n, nb),
        out_shape=jax.ShapeDtypeStruct((rows, half), BF16),
        in_specs=[hbm] * 9,
        out_specs=vmem,
        scratch_shapes=[
            vm((rows, width), BF16), vm((rows, width), BF16),
            vm((width, cols), BF16), vm((width, cols), BF16), vm((width, cols), BF16),
            vm((cols, width), BF16), pltpu.SMEM(adjacency.shape, jnp.int32),
            pltpu.SMEM(adjacency.shape, jnp.int32), vm((1, rows), jnp.int32), dma((9,)),
            vm((rows, rows), BF16),
            vm((2, rows, half), BF16), vm((2, rows, half), BF16),
            vm((n, 2, rows, half), BF16), vm((n, 2, rows, half), BF16),
            vm((rows, cols), BF16), vm((rows, cols), BF16), vm((2, cols, keys), BF16),
            vm((2, lanes, cols), BF16), vm((2, lanes, cols), BF16),
            vm((n, 2, lanes, cols), BF16),
            vm((2, rows, lanes), F32), vm((2, rows, lanes), F32),
            vm((n, 2, block, lanes), F32), vm((n, 2, block, lanes), F32),
            vm((n, 2, block, lanes), F32), vm((2, keys, lanes), BF16),
            vm((2, 8, lanes), F32), vm((n, 2, 8, lanes), F32),
            vm((2, 8, 128), F32), vm((2, 8, 128), F32), vm((n, 2, 8, 128), F32), vm((2, 8, 128), F32),
            vm((cols, rows), F32), vm((rows, cols), F32), vm((rows, cols), F32),
            vm((rows, half), BF16), vm((rows, half), BF16),
        ] + [dma((n + 1,)), dma((n + 1,)), dma((n,)), dma((n,))] * 2
        + [dma((n + 1,)), dma((n + 1,)), dma(()), dma(()), dma((2,)), vm((2, rows, half), F32)]
        + [pltpu.SemaphoreType.REGULAR((n + 1,))],
        compiler_params=pltpu.CompilerParams(
            collective_id=0, has_side_effects=True, vmem_limit_bytes=63 * 1024 * 1024
        ),
    )(
        features, cotangent, w_query, w_key, w_value, w_out,
        adjacency, partner.T, node_order.reshape(1, rows),
    )


def solution(mesh):
    rows = P(("parts", "slab", "blk"), None)
    in_specs = (
        rows, rows,
        P(None, "head"), P(None, "head"), P(None, "head"), P("head", None),
        rows, P(None, ("parts", "slab", "blk")), P(("parts", "slab", "blk")),
    )
    return jax.shard_map(
        body, mesh=mesh, in_specs=in_specs,
        out_specs=P(("parts", "slab", "blk"), "head"), check_vma=False,
    )
```

```python
import functools

import jax
import jax.numpy as jnp
from jax import lax
from jax.experimental import pallas as pl
from jax.experimental.pallas import tpu as pltpu
from jax.sharding import PartitionSpec as P

HEAD_DIM = 64
OFF = -1e30
NT = (((1,), (1,)), ((), ()))
TN = (((0,), (0,)), ((), ()))
F32, BF16 = jnp.float32, jnp.bfloat16
MESH = pl.DeviceIdType.MESH


def mm(a, b):
    return jnp.dot(a, b, preferred_element_type=F32)


def mm_nt(a, b):
    return lax.dot_general(a, b, NT, preferred_element_type=F32)


def kernel(
    n, nb,
    feat_hbm, cot_hbm, w_q_hbm, w_k_hbm, w_v_hbm, w_o_hbm, adj_hbm, part_hbm, order_hbm, out,
    feat, cot, w_q, w_k, w_v, w_o, adj, part, order, fetch,
    own_x, own_c, rx, rc, k_own, v_own, kt_all, qm_own, gm_own,
    qm_far, gm_far, gp_far, e_own, g_own, e_far, g_far, s_back, ds_all, rows_own, rows_far,
    stat, stat_near, stat_twin, stat_far,
    dk, dv, part_out, give, take,
    x_send, x_recv, c_send, c_recv, t_send, t_recv, w_send, w_recv, h_send, h_recv, hop_send, acks,
):
    rows, width = feat.shape
    half = width // 2
    cols = w_q.shape[2]
    groups = 2
    heads = cols // HEAD_DIM
    block = rows // 2
    lanes = heads * block
    scale = HEAD_DIM ** -0.5
    NEAR, TWIN = 0, n
    h, slab, x = (lax.axis_index(a) for a in ("head", "slab", "blk"))
    twin = {"head": 1 - h}
    near = {"blk": lax.rem(x + jnp.where(h == 0, nb - 1, 1), nb), "head": 1 - h}

    def onward(d):
        return {"slab": lax.rem(slab + d, n)}

    line = n == 4 and nb == 2
    at_start, at_end = slab == 0, slab == n - 1
    inner = jnp.logical_and(slab > 0, slab < n - 1)

    def each(f):
        if n <= 4:
            for d in range(1, n):
                f(d)
        else:
            lax.fori_loop(1, n, lambda d, c: (f(d), c)[1], 0)

    def slots(f):
        f(TWIN)
        f(NEAR)
        each(f)

    def each_direct(f):
        if line:
            f(2)
            pl.when(jnp.logical_not(at_end))(lambda: f(1))
            pl.when(jnp.logical_not(at_start))(lambda: f(3))
        else:
            each(f)

    weights = (w_q, w_k, w_v, w_o)
    loads = [
        pltpu.make_async_copy(src, dst, fetch.at[i])
        for i, (src, dst) in enumerate((
            (order_hbm, order), (feat_hbm, feat), (cot_hbm, cot), (w_q_hbm, w_q.at[h]),
            (w_k_hbm, w_k.at[h]), (w_v_hbm, w_v.at[h]), (w_o_hbm, w_o.at[h]),
            (adj_hbm, adj), (part_hbm, part),
        ))
    ]
    for load in loads:
        load.start()
    barrier = pltpu.get_barrier_semaphore()

    def greet(where):
        pl.semaphore_signal(barrier, inc=1, device_id=where, device_id_type=MESH)

    def ack(where, k):
        pl.semaphore_signal(acks.at[k], inc=1, device_id=where, device_id_type=MESH)

    def answered(k):
        pl.semaphore_wait(acks.at[k], 1)

    if line:
        pl.when(h == 0)(lambda: greet(twin))
        pl.when(x == 0)(lambda: greet(near))
        for d in range(1, n):
            pl.when(slab + d < n)(lambda d=d: greet({"slab": slab + d}))
    else:
        greet(near)
        greet(twin)
        each(lambda d: greet(onward(d)))

    def enter():
        if line:
            earlier = slab + x + h
            pl.when(earlier > 0)(lambda: pl.semaphore_wait(barrier, earlier))
            for d in range(1, n):
                pl.when(slab >= d)(lambda d=d: ack({"slab": slab - d}, d))
            pl.when(x == 1)(lambda: ack(near, NEAR))
            pl.when(h == 1)(lambda: ack(twin, TWIN))
        else:
            pl.semaphore_wait(barrier, n + 1)

    def copy(src, dst, send, recv, where):
        return pltpu.make_async_remote_copy(
            src_ref=src, dst_ref=dst, send_sem=send, recv_sem=recv,
            device_id=where, device_id_type=MESH,
        )

    def slot_copy(own, far, send, recv, i):
        where = near if isinstance(i, int) and i == NEAR else twin if isinstance(i, int) and i == TWIN else onward(i)
        return copy(own, far.at[i], send.at[i], recv.at[i], where)

    x_slot = functools.partial(slot_copy, own_x, rx, x_send, x_recv)
    c_slot = functools.partial(slot_copy, own_c, rc, c_send, c_recv)

    def stat_slot(i):
        own = stat
        if isinstance(i, int) and i in (NEAR, TWIN):
            own = stat_near if i == NEAR else stat_twin
        return slot_copy(own, stat_far, t_send, t_recv, i)

    def hop_copy(far, recv, k):
        up = slab == n - 2
        slot = jnp.where(up, 3, 1)
        return copy(
            far.at[2], far.at[slot], hop_send.at[k], recv.at[slot],
            {"slab": jnp.where(up, n - 1, 0)},
        )

    x_hop = functools.partial(hop_copy, rx, x_recv, 0)
    c_hop = functools.partial(hop_copy, rc, c_recv, 1)

    w_copies = [
        copy(w.at[h], w.at[h], w_send.at[i], w_recv.at[i], twin) for i, w in enumerate(weights)
    ]

    def send_slab(copy_of, plan, wait=False):
        for z, ds in plan.items():
            @pl.when(slab == z)
            def _(z=z, ds=ds):
                for d in ds:
                    if wait and z + d < n:
                        answered(d)
                    copy_of(d).start()

    loads[0].wait()
    loads[1].wait()

    def picked(b):
        places = order[:, pl.ds(pl.multiple_of(b * block, block), block)]
        hot = lax.broadcasted_iota(jnp.int32, (rows, block), 0) == places
        return jnp.where(hot, 1.0, 0.0).astype(BF16)

    pick = picked(h)
    own_x[...] = lax.dot_general(pick, feat[...], TN, preferred_element_type=F32).astype(BF16)

    enter()
    if line:
        send_slab(x_slot, {0: (1, 2), 1: (3, 1, 2), 2: (2, 3, 1), 3: (2, 3)}, wait=True)
        pl.when(x == 0)(lambda: answered(NEAR))
        pl.when(h == 0)(lambda: answered(TWIN))
    else:
        each_direct(lambda d: x_slot(d).start())
    x_slot(NEAR).start()
    x_slot(TWIN).start()

    loads[2].wait()
    own_c[...] = lax.dot_general(pick, cot[...], TN, preferred_element_type=F32).astype(BF16)
    if line:
        send_slab(c_slot, {0: (1, 2), 1: (3,), 2: (2, 3, 1), 3: (2, 3)})
    else:
        each_direct(lambda d: c_slot(d).start())
    c_slot(NEAR).start()
    c_slot(TWIN).start()

    for i in range(4):
        loads[3 + i].wait()
        w_copies[i].start()
    for load in loads[7:]:
        load.wait()

    lane_head = lax.broadcasted_iota(jnp.int32, (1, cols), 1) // HEAD_DIM
    masks = [jnp.where(lane_head == i, 1.0, 0.0).astype(BF16) for i in range(heads)]

    def masked(value):
        return jnp.concatenate([value * mask for mask in masks], axis=0)

    def weight_flag(flag):
        return jnp.where(flag > 0, 1.0, 0.0).astype(F32)

    def flag_of(i):
        return weight_flag(adj[h, 2 * h] if i == NEAR else adj[h, 2 - 2 * h])

    def far_weight(i):
        if isinstance(i, int) and i in (NEAR, TWIN):
            return flag_of(i)
        source = lax.rem(slab + n - i, n)
        total = jnp.float32(0.0)
        for m in range(3):
            total = total + jnp.where(lax.div(part[h, m], 2 * nb) == source, 1.0, 0.0)
        return total

    def bias(w):
        return jnp.where(w > 0.0, 0.0, OFF).astype(F32)

    def key_cols(i):
        if isinstance(i, int):
            return pl.ds(i * block, block)
        return pl.ds(pl.multiple_of(i * block, block), block)

    for w_copy in w_copies:
        w_copy.wait_recv()

    xs, cs = own_x[...], own_c[...]
    for a in range(groups):
        q = (mm(xs, w_q[a]).astype(BF16) * scale).astype(BF16)
        k32 = mm(xs, w_k[a])
        k = k32.astype(BF16)
        v = mm(xs, w_v[a]).astype(BF16)
        qm, gm = masked(q), masked(mm_nt(cs, w_o[a]).astype(BF16))
        k_own[a] = k
        v_own[a] = v
        kt_all[a, :, key_cols(n + 1)] = k32.T.astype(BF16)
        qm_own[a] = qm
        gm_own[a] = gm
        s = mm_nt(k, qm)
        g = mm_nt(v, gm)
        top = jnp.max(s, axis=0, keepdims=True)
        e = jnp.exp(s - top)
        e_own[a] = e
        g_own[a] = g
        rows_own[a, 0:1] = top
        rows_own[a, 1:2] = jnp.sum(e, axis=0, keepdims=True)
        rows_own[a, 2:3] = jnp.sum(e * g, axis=0, keepdims=True)

    def forward_slot(i):
        xi = rx[i]
        for a in range(groups):
            q = (mm(xi, w_q[a]).astype(BF16) * scale).astype(BF16)
            k32 = mm(xi, w_k[a])
            v = mm(xi, w_v[a]).astype(BF16)
            kt_all[a, :, key_cols(i)] = k32.T.astype(BF16)
            qm = masked(q)
            qm_far[i, a] = qm
            s = mm_nt(k32.astype(BF16), qm_own[a])
            g = mm_nt(v, gm_own[a])
            top = jnp.max(s, axis=0, keepdims=True)
            e = jnp.exp(s - top)
            e_far[i, a] = e
            g_far[i, a] = g
            rows_far[i, a, 0:1] = top
            rows_far[i, a, 1:2] = jnp.sum(e, axis=0, keepdims=True)
            rows_far[i, a, 2:3] = jnp.sum(e * g, axis=0, keepdims=True)
            s_back[i, a] = mm_nt(k_own[a], qm)

    def kept(i):
        return i if line else 0

    def value_slot(i):
        ci = rc[i]
        for a in range(groups):
            gm = masked(mm_nt(ci, w_o[a]).astype(BF16))
            gm_far[kept(i), a] = gm
            gp_far[kept(i), a] = mm_nt(v_own[a], gm)

    first, last = (jnp.where(at_start, 3, 1), jnp.where(at_start, 1, 3)) if line else (None, None)

    def arrive(copy_of, hop, i):
        copy_of(i).wait_recv()
        if hop is not None:
            @pl.when(inner)
            def _():
                hop().start()

    x_slot(TWIN).wait_recv()
    forward_slot(TWIN)
    x_slot(NEAR).wait_recv()
    forward_slot(NEAR)
    if line:
        arrive(x_slot, None, first)
        forward_slot(first)
        c_slot(TWIN).wait_recv()
        value_slot(TWIN)
        arrive(x_slot, x_hop, 2)
        send_slab(c_slot, {1: (1, 2)})
        forward_slot(2)
        c_slot(NEAR).wait_recv()
        value_slot(NEAR)
        arrive(x_slot, None, last)
        forward_slot(last)
    else:
        def step(d):
            arrive(x_slot, None, d)
            forward_slot(d)

        each(step)

    tiles = lanes // 128

    def pack(ref, at, top, dot):
        for j in range(tiles):
            part_cols = slice(j * 128, (j + 1) * 128)
            ref[at, j:j + 1, :] = top[:, part_cols]
            ref[at, tiles + j:tiles + j + 1, :] = dot[:, part_cols]

    def unpack(tile):
        return (
            jnp.concatenate([tile[j:j + 1, :] for j in range(tiles)], axis=1),
            jnp.concatenate([tile[tiles + j:tiles + j + 1, :] for j in range(tiles)], axis=1),
        )

    for a in range(groups):
        rows_own[a, 3:4] = rows_own[a, 0:1]

        def far_top(i):
            rows_own[a, 3:4] = jnp.maximum(
                rows_own[a, 3:4], rows_far[i, a, 0:1] + bias(far_weight(i))
            )

        slots(far_top)
        top = rows_own[a, 3:4]
        share_own = jnp.exp(rows_own[a, 0:1] - top)
        rows_own[a, 4:5] = rows_own[a, 1:2] * share_own
        rows_own[a, 5:6] = rows_own[a, 2:3] * share_own

        def far_sum(i):
            w = far_weight(i)
            f = w * jnp.exp(rows_far[i, a, 0:1] + (bias(w) - top))
            rows_far[i, a, 3:4] = f
            rows_own[a, 4:5] += f * rows_far[i, a, 1:2]
            rows_own[a, 5:6] += f * rows_far[i, a, 2:3]

        slots(far_sum)
        inverse = 1.0 / rows_own[a, 4:5]
        dot = rows_own[a, 5:6] * inverse
        row_total = top + jnp.log(rows_own[a, 4:5])
        rows_own[a, 3:4] = share_own * inverse
        rows_own[a, 4:5] = inverse
        rows_own[a, 5:6] = dot
        pack(stat, a, row_total, dot)
        pack(stat_near, a, jnp.where(flag_of(NEAR) > 0.0, row_total, -OFF), dot)
        pack(stat_twin, a, jnp.where(flag_of(TWIN) > 0.0, row_total, -OFF), dot)

    if line:
        pl.when(at_start)(lambda: answered(3))
    each(lambda d: stat_slot(d).start())
    stat_slot(NEAR).start()
    stat_slot(TWIN).start()

    if line:
        arrive(c_slot, None, first)
        arrive(c_slot, c_hop, 2)

    def half_at(which):
        return pl.ds(pl.multiple_of(which * half, half), half)

    for a in range(groups):
        p = e_own[a] * rows_own[a, 3:4]
        ds = (p * (g_own[a] - rows_own[a, 5:6])).astype(BF16)
        ds_all[a, key_cols(n + 1)] = ds
        dv[a] = mm(p.astype(BF16), gm_own[a])
        dk[a] = mm(ds, qm_own[a])

        def query_grad(i):
            f = rows_far[i, a, 3:4] * rows_own[a, 4:5]
            ds_all[a, key_cols(i)] = (
                e_far[i, a] * f * (g_far[i, a] - rows_own[a, 5:6])
            ).astype(BF16)

        slots(query_grad)
        dq = jnp.concatenate([
            mm(kt_all[a, j * HEAD_DIM:(j + 1) * HEAD_DIM, :], ds_all[a, :, j * block:(j + 1) * block])
            for j in range(heads)
        ], axis=0)
        dq_low = (dq.T * scale).astype(BF16)
        for k, which in enumerate((1 - h, h)):
            piece = mm_nt(dq_low, w_q[a, half_at(which), :])
            if a == 0:
                part_out[k] = piece
            else:
                part_out[k] += piece

    def weigh_slot(i):
        for a in range(groups):
            row_total, dot = unpack(stat_far[i, a])
            if isinstance(i, int) and i in (NEAR, TWIN):
                p = jnp.exp(s_back[i, a] - row_total)
            else:
                w = far_weight(i)
                p = jnp.exp(s_back[i, a] - jnp.where(w > 0.0, row_total, -OFF)) * w
            ds = (p * (gp_far[kept(i), a] - dot)).astype(BF16)
            dv[a] += mm(p.astype(BF16), gm_far[kept(i), a])
            dk[a] += mm(ds, qm_far[i, a])

    if line:
        value_slot(first)
        value_slot(2)
        for i in (TWIN, NEAR, first, 2):
            stat_slot(i).wait_recv()
            weigh_slot(i)
        arrive(c_slot, None, last)
        value_slot(last)
        stat_slot(last).wait_recv()
        weigh_slot(last)
    else:
        for i in (TWIN, NEAR):
            c_slot(i).wait_recv()
            value_slot(i)
            stat_slot(i).wait_recv()
            weigh_slot(i)

        def back_step(d):
            arrive(c_slot, None, d)
            value_slot(d)
            stat_slot(d).wait_recv()
            weigh_slot(d)

        each(back_step)

    dk_low = [dk[a].astype(BF16) for a in range(groups)]
    dv_low = [dv[a].astype(BF16) for a in range(groups)]

    def share(k, which):
        at = half_at(which)
        total = part_out[k]
        for a in range(groups):
            total = total + mm_nt(dk_low[a], w_k[a, at, :]) + mm_nt(dv_low[a], w_v[a, at, :])
        return total.astype(BF16)

    give[...] = share(0, 1 - h)
    swap = copy(give, take, h_send, h_recv, twin)
    swap.start()
    mine = mm(pick, share(1, h))
    pick_twin = picked(1 - h)
    swap.wait_recv()
    out[...] = (mine + mm(pick_twin, take[...])).astype(BF16)

    swap.wait_send()
    for i in (NEAR, TWIN):
        for copy_of in (x_slot, c_slot, stat_slot):
            copy_of(i).wait_send()
    for w_copy in w_copies:
        w_copy.wait_send()
    each(lambda d: stat_slot(d).wait_send())
    each_direct(lambda d: x_slot(d).wait_send())
    each_direct(lambda d: c_slot(d).wait_send())
    if line:
        @pl.when(inner)
        def _():
            x_hop().wait_send()
            c_hop().wait_send()


def body(features, cotangent, w_query, w_key, w_value, w_out, adjacency, partner, node_order):
    n, nb = lax.axis_size("slab"), lax.axis_size("blk")
    rows, width = features.shape
    cols = w_query.shape[1]
    half, block = width // 2, rows // 2
    lanes = (cols // HEAD_DIM) * block
    far = n + 1
    keys = (n + 2) * block
    kept = far if n == 4 and nb == 2 else 1
    vm, dma = pltpu.VMEM, pltpu.SemaphoreType.DMA
    vmem, hbm = (pl.BlockSpec(memory_space=m) for m in (pltpu.VMEM, pltpu.HBM))
    return pl.pallas_call(
        functools.partial(kernel, n, nb),
        out_shape=jax.ShapeDtypeStruct((rows, half), BF16),
        in_specs=[hbm] * 9,
        out_specs=vmem,
        scratch_shapes=[
            vm((rows, width), BF16), vm((rows, width), BF16),
            vm((2, width, cols), BF16), vm((2, width, cols), BF16), vm((2, width, cols), BF16),
            vm((2, cols, width), BF16), pltpu.SMEM(adjacency.shape, jnp.int32),
            pltpu.SMEM(adjacency.shape, jnp.int32), vm((1, rows), jnp.int32), dma((9,)),
            vm((block, width), BF16), vm((block, width), BF16),
            vm((far, block, width), BF16), vm((far, block, width), BF16),
            vm((2, block, cols), BF16), vm((2, block, cols), BF16), vm((2, cols, keys), BF16),
            vm((2, lanes, cols), BF16), vm((2, lanes, cols), BF16),
            vm((far, 2, lanes, cols), BF16), vm((kept, 2, lanes, cols), BF16),
            vm((kept, 2, block, lanes), F32),
            vm((2, block, lanes), F32), vm((2, block, lanes), F32),
            vm((far, 2, block, lanes), F32), vm((far, 2, block, lanes), F32),
            vm((far, 2, block, lanes), F32), vm((2, keys, lanes), BF16),
            vm((2, 8, lanes), F32), vm((far, 2, 8, lanes), F32),
            vm((2, 8, 128), F32), vm((2, 8, 128), F32), vm((2, 8, 128), F32), vm((far, 2, 8, 128), F32),
            vm((2, block, cols), F32), vm((2, block, cols), F32), vm((2, block, half), F32),
            vm((block, half), BF16), vm((block, half), BF16),
        ] + [dma((far,)) for _ in range(6)]
        + [dma((4,)), dma((4,)), dma(()), dma(()), dma((2,)), pltpu.SemaphoreType.REGULAR((far,))],
        compiler_params=pltpu.CompilerParams(
            collective_id=0, has_side_effects=True, vmem_limit_bytes=(40 if n <= 4 else 63) * 1024 * 1024
        ),
    )(*(
        pltpu.with_memory_space_constraint(v, pltpu.HBM) for v in (
            features, cotangent, w_query, w_key, w_value, w_out,
            adjacency, partner.T, node_order.reshape(1, rows),
        )
    ))


def solution(mesh):
    rows = P(("parts", "slab", "blk"), None)
    in_specs = (
        rows, rows,
        P(None, "head"), P(None, "head"), P(None, "head"), P("head", None),
        rows, P(None, ("parts", "slab", "blk")), P(("parts", "slab", "blk")),
    )
    return jax.shard_map(
        body, mesh=mesh, in_specs=in_specs,
        out_specs=P(("parts", "slab", "blk"), "head"), check_vma=False,
    )
```

```python
import functools

import jax
import jax.numpy as jnp
from jax import lax
from jax.experimental import pallas as pl
from jax.experimental.pallas import tpu as pltpu
from jax.sharding import PartitionSpec as P

HEAD_DIM = 64
OFF = -1e30
NT = (((1,), (1,)), ((), ()))
TN = (((0,), (0,)), ((), ()))
F32, BF16 = jnp.float32, jnp.bfloat16
MESH = pl.DeviceIdType.MESH


def mm(a, b):
    return jnp.dot(a, b, preferred_element_type=F32)


def mm_nt(a, b):
    return lax.dot_general(a, b, NT, preferred_element_type=F32)


def kernel(
    n, nb,
    feat_hbm, cot_hbm, w_q_hbm, w_k_hbm, w_v_hbm, w_o_hbm, adj_hbm, part_hbm, order_hbm, out,
    feat, cot, w_q, w_k, w_v, w_o, adj, part, order, fetch,
    own_x, own_c, rx, rc, k_own, v_own, kt_all, qm_own, gm_own,
    qm_far, gm_far, gp_far, e_own, g_own, e_far, g_far, s_back, ds_all, rows_own, rows_far,
    stat, stat_near, stat_twin, stat_far,
    dk, dv, part_out, give, take,
    x_send, x_recv, c_send, c_recv, t_send, t_recv, w_send, w_recv, h_send, h_recv, hop_send, acks,
):
    rows, width = feat.shape
    half = width // 2
    cols = w_q.shape[2]
    groups = 2
    heads = cols // HEAD_DIM
    block = rows // 2
    lanes = heads * block
    scale = HEAD_DIM ** -0.5
    NEAR, TWIN = 0, n
    h, slab, x = (lax.axis_index(a) for a in ("head", "slab", "blk"))
    twin = {"head": 1 - h}
    near = {"blk": lax.rem(x + jnp.where(h == 0, nb - 1, 1), nb), "head": 1 - h}

    def onward(d):
        return {"slab": lax.rem(slab + d, n)}

    line = n == 4 and nb == 2
    at_start, at_end = slab == 0, slab == n - 1
    inner = jnp.logical_and(slab > 0, slab < n - 1)

    def each(f):
        if n <= 4:
            for d in range(1, n):
                f(d)
        else:
            lax.fori_loop(1, n, lambda d, c: (f(d), c)[1], 0)

    def slots(f):
        f(TWIN)
        f(NEAR)
        each(f)

    def each_direct(f):
        if line:
            f(2)
            pl.when(jnp.logical_not(at_end))(lambda: f(1))
            pl.when(jnp.logical_not(at_start))(lambda: f(3))
        else:
            each(f)

    weights = (w_q, w_k, w_v, w_o)
    loads = [
        pltpu.make_async_copy(src, dst, fetch.at[i])
        for i, (src, dst) in enumerate((
            (order_hbm, order), (feat_hbm, feat), (cot_hbm, cot), (w_q_hbm, w_q.at[h]),
            (w_k_hbm, w_k.at[h]), (w_v_hbm, w_v.at[h]), (w_o_hbm, w_o.at[h]),
            (adj_hbm, adj), (part_hbm, part),
        ))
    ]
    for load in loads:
        load.start()
    barrier = pltpu.get_barrier_semaphore()

    def greet(where):
        pl.semaphore_signal(barrier, inc=1, device_id=where, device_id_type=MESH)

    def ack(where, k):
        pl.semaphore_signal(acks.at[k], inc=1, device_id=where, device_id_type=MESH)

    def answered(k):
        pl.semaphore_wait(acks.at[k], 1)

    if line:
        pl.when(h == 0)(lambda: greet(twin))
        pl.when(x == 0)(lambda: greet(near))
        for d in range(1, n):
            pl.when(slab + d < n)(lambda d=d: greet({"slab": slab + d}))
    else:
        greet(near)
        greet(twin)
        each(lambda d: greet(onward(d)))

    def enter():
        if line:
            earlier = slab + x + h
            pl.when(earlier > 0)(lambda: pl.semaphore_wait(barrier, earlier))
            for d in range(1, n):
                pl.when(slab >= d)(lambda d=d: ack({"slab": slab - d}, d))
            pl.when(x == 1)(lambda: ack(near, NEAR))
            pl.when(h == 1)(lambda: ack(twin, TWIN))
        else:
            pl.semaphore_wait(barrier, n + 1)

    def copy(src, dst, send, recv, where):
        return pltpu.make_async_remote_copy(
            src_ref=src, dst_ref=dst, send_sem=send, recv_sem=recv,
            device_id=where, device_id_type=MESH,
        )

    def slot_copy(own, far, send, recv, i):
        where = near if isinstance(i, int) and i == NEAR else twin if isinstance(i, int) and i == TWIN else onward(i)
        return copy(own, far.at[i], send.at[i], recv.at[i], where)

    x_slot = functools.partial(slot_copy, own_x, rx, x_send, x_recv)
    c_slot = functools.partial(slot_copy, own_c, rc, c_send, c_recv)

    def stat_slot(i):
        own = stat
        if isinstance(i, int) and i in (NEAR, TWIN):
            own = stat_near if i == NEAR else stat_twin
        return slot_copy(own, stat_far, t_send, t_recv, i)

    def hop_copy(far, recv, k):
        up = slab == n - 2
        slot = jnp.where(up, 3, 1)
        return copy(
            far.at[2], far.at[slot], hop_send.at[k], recv.at[slot],
            {"slab": jnp.where(up, n - 1, 0)},
        )

    x_hop = functools.partial(hop_copy, rx, x_recv, 0)
    c_hop = functools.partial(hop_copy, rc, c_recv, 1)

    w_copies = [
        copy(w.at[h], w.at[h], w_send.at[i], w_recv.at[i], twin) for i, w in enumerate(weights)
    ]

    def send_slab(copy_of, plan, wait=False):
        for z, ds in plan.items():
            @pl.when(slab == z)
            def _(z=z, ds=ds):
                for d in ds:
                    if wait and z + d < n:
                        answered(d)
                    copy_of(d).start()

    loads[0].wait()
    loads[1].wait()

    def picked(b):
        places = order[:, pl.ds(pl.multiple_of(b * block, block), block)]
        hot = lax.broadcasted_iota(jnp.int32, (rows, block), 0) == places
        return jnp.where(hot, 1.0, 0.0).astype(BF16)

    pick = picked(h)
    own_x[...] = lax.dot_general(pick, feat[...], TN, preferred_element_type=F32).astype(BF16)

    enter()
    if line:
        send_slab(x_slot, {0: (1, 2), 1: (3, 1, 2), 2: (2, 1, 3), 3: (2, 3)}, wait=True)
        pl.when(x == 0)(lambda: answered(NEAR))
        pl.when(h == 0)(lambda: answered(TWIN))
    else:
        each_direct(lambda d: x_slot(d).start())
    x_slot(NEAR).start()
    x_slot(TWIN).start()

    loads[2].wait()
    own_c[...] = lax.dot_general(pick, cot[...], TN, preferred_element_type=F32).astype(BF16)
    if line:
        send_slab(c_slot, {0: (1, 2), 1: (3,), 2: (2, 1), 3: (3, 2)})
    else:
        each_direct(lambda d: c_slot(d).start())
    c_slot(NEAR).start()
    c_slot(TWIN).start()

    for i in range(4):
        loads[3 + i].wait()
        w_copies[i].start()
    for load in loads[7:]:
        load.wait()

    lane_head = lax.broadcasted_iota(jnp.int32, (1, cols), 1) // HEAD_DIM
    masks = [jnp.where(lane_head == i, 1.0, 0.0).astype(BF16) for i in range(heads)]

    def masked(value):
        return jnp.concatenate([value * mask for mask in masks], axis=0)

    def weight_flag(flag):
        return jnp.where(flag > 0, 1.0, 0.0).astype(F32)

    def flag_of(i):
        return weight_flag(adj[h, 2 * h] if i == NEAR else adj[h, 2 - 2 * h])

    def far_weight(i):
        if isinstance(i, int) and i in (NEAR, TWIN):
            return flag_of(i)
        source = lax.rem(slab + n - i, n)
        total = jnp.float32(0.0)
        for m in range(3):
            total = total + jnp.where(lax.div(part[h, m], 2 * nb) == source, 1.0, 0.0)
        return total

    def bias(w):
        return jnp.where(w > 0.0, 0.0, OFF).astype(F32)

    def key_cols(i):
        if isinstance(i, int):
            return pl.ds(i * block, block)
        return pl.ds(pl.multiple_of(i * block, block), block)

    for w_copy in w_copies:
        w_copy.wait_recv()

    xs, cs = own_x[...], own_c[...]
    for a in range(groups):
        q = (mm(xs, w_q[a]).astype(BF16) * scale).astype(BF16)
        k32 = mm(xs, w_k[a])
        k = k32.astype(BF16)
        v = mm(xs, w_v[a]).astype(BF16)
        qm, gm = masked(q), masked(mm_nt(cs, w_o[a]).astype(BF16))
        k_own[a] = k
        v_own[a] = v
        kt_all[a, :, key_cols(n + 1)] = k32.T.astype(BF16)
        qm_own[a] = qm
        gm_own[a] = gm
        s = mm_nt(k, qm)
        g = mm_nt(v, gm)
        top = jnp.max(s, axis=0, keepdims=True)
        e = jnp.exp(s - top)
        e_own[a] = e
        g_own[a] = g
        rows_own[a, 0:1] = top
        rows_own[a, 1:2] = jnp.sum(e, axis=0, keepdims=True)
        rows_own[a, 2:3] = jnp.sum(e * g, axis=0, keepdims=True)

    def forward_slot(i):
        xi = rx[i]
        for a in range(groups):
            q = (mm(xi, w_q[a]).astype(BF16) * scale).astype(BF16)
            k32 = mm(xi, w_k[a])
            v = mm(xi, w_v[a]).astype(BF16)
            kt_all[a, :, key_cols(i)] = k32.T.astype(BF16)
            qm = masked(q)
            qm_far[i, a] = qm
            s = mm_nt(k32.astype(BF16), qm_own[a])
            g = mm_nt(v, gm_own[a])
            top = jnp.max(s, axis=0, keepdims=True)
            e = jnp.exp(s - top)
            e_far[i, a] = e
            g_far[i, a] = g
            rows_far[i, a, 0:1] = top
            rows_far[i, a, 1:2] = jnp.sum(e, axis=0, keepdims=True)
            rows_far[i, a, 2:3] = jnp.sum(e * g, axis=0, keepdims=True)
            s_back[i, a] = mm_nt(k_own[a], qm)

    def kept(i):
        return i if line else 0

    def value_slot(i):
        ci = rc[i]
        for a in range(groups):
            gm = masked(mm_nt(ci, w_o[a]).astype(BF16))
            gm_far[kept(i), a] = gm
            gp_far[kept(i), a] = mm_nt(v_own[a], gm)

    first, last = (jnp.where(at_start, 3, 1), jnp.where(at_start, 1, 3)) if line else (None, None)

    def arrive(copy_of, hop, i):
        copy_of(i).wait_recv()
        if hop is not None:
            @pl.when(inner)
            def _():
                hop().start()

    x_slot(TWIN).wait_recv()
    forward_slot(TWIN)
    x_slot(NEAR).wait_recv()
    forward_slot(NEAR)
    if line:
        arrive(x_slot, None, first)
        forward_slot(first)
        c_slot(TWIN).wait_recv()
        value_slot(TWIN)
        arrive(x_slot, x_hop, 2)
        send_slab(c_slot, {1: (1, 2), 2: (3,)})
        forward_slot(2)
        c_slot(NEAR).wait_recv()
        value_slot(NEAR)
        arrive(x_slot, None, last)
        forward_slot(last)
    else:
        def step(d):
            arrive(x_slot, None, d)
            forward_slot(d)

        each(step)

    tiles = lanes // 128

    def pack(ref, at, top, dot):
        for j in range(tiles):
            part_cols = slice(j * 128, (j + 1) * 128)
            ref[at, j:j + 1, :] = top[:, part_cols]
            ref[at, tiles + j:tiles + j + 1, :] = dot[:, part_cols]

    def unpack(tile):
        return (
            jnp.concatenate([tile[j:j + 1, :] for j in range(tiles)], axis=1),
            jnp.concatenate([tile[tiles + j:tiles + j + 1, :] for j in range(tiles)], axis=1),
        )

    for a in range(groups):
        rows_own[a, 3:4] = rows_own[a, 0:1]

        def far_top(i):
            rows_own[a, 3:4] = jnp.maximum(
                rows_own[a, 3:4], rows_far[i, a, 0:1] + bias(far_weight(i))
            )

        slots(far_top)
        top = rows_own[a, 3:4]
        share_own = jnp.exp(rows_own[a, 0:1] - top)
        rows_own[a, 4:5] = rows_own[a, 1:2] * share_own
        rows_own[a, 5:6] = rows_own[a, 2:3] * share_own

        def far_sum(i):
            w = far_weight(i)
            f = w * jnp.exp(rows_far[i, a, 0:1] + (bias(w) - top))
            rows_far[i, a, 3:4] = f
            rows_own[a, 4:5] += f * rows_far[i, a, 1:2]
            rows_own[a, 5:6] += f * rows_far[i, a, 2:3]

        slots(far_sum)
        inverse = 1.0 / rows_own[a, 4:5]
        dot = rows_own[a, 5:6] * inverse
        row_total = top + jnp.log(rows_own[a, 4:5])
        rows_own[a, 3:4] = share_own * inverse
        rows_own[a, 4:5] = inverse
        rows_own[a, 5:6] = dot
        pack(stat, a, row_total, dot)
        pack(stat_near, a, jnp.where(flag_of(NEAR) > 0.0, row_total, -OFF), dot)
        pack(stat_twin, a, jnp.where(flag_of(TWIN) > 0.0, row_total, -OFF), dot)

    if line:
        pl.when(at_start)(lambda: answered(3))
    each(lambda d: stat_slot(d).start())
    stat_slot(NEAR).start()
    stat_slot(TWIN).start()

    if line:
        arrive(c_slot, None, first)
        arrive(c_slot, c_hop, 2)

    def half_at(which):
        return pl.ds(pl.multiple_of(which * half, half), half)

    for a in range(groups):
        p = e_own[a] * rows_own[a, 3:4]
        ds = (p * (g_own[a] - rows_own[a, 5:6])).astype(BF16)
        ds_all[a, key_cols(n + 1)] = ds
        dv[a] = mm(p.astype(BF16), gm_own[a])
        dk[a] = mm(ds, qm_own[a])

        def query_grad(i):
            f = rows_far[i, a, 3:4] * rows_own[a, 4:5]
            ds_all[a, key_cols(i)] = (
                e_far[i, a] * f * (g_far[i, a] - rows_own[a, 5:6])
            ).astype(BF16)

        slots(query_grad)
        dq = jnp.concatenate([
            mm(kt_all[a, j * HEAD_DIM:(j + 1) * HEAD_DIM, :], ds_all[a, :, j * block:(j + 1) * block])
            for j in range(heads)
        ], axis=0)
        dq_low = (dq.T * scale).astype(BF16)
        for k, which in enumerate((1 - h, h)):
            piece = mm_nt(dq_low, w_q[a, half_at(which), :])
            if a == 0:
                part_out[k] = piece
            else:
                part_out[k] += piece

    def weigh_slot(i):
        for a in range(groups):
            row_total, dot = unpack(stat_far[i, a])
            if isinstance(i, int) and i in (NEAR, TWIN):
                p = jnp.exp(s_back[i, a] - row_total)
            else:
                w = far_weight(i)
                p = jnp.exp(s_back[i, a] - jnp.where(w > 0.0, row_total, -OFF)) * w
            ds = (p * (gp_far[kept(i), a] - dot)).astype(BF16)
            dv[a] += mm(p.astype(BF16), gm_far[kept(i), a])
            dk[a] += mm(ds, qm_far[i, a])

    if line:
        value_slot(first)
        value_slot(2)
        for i in (TWIN, NEAR, first, 2):
            stat_slot(i).wait_recv()
        for i in (TWIN, NEAR, first, 2):
            weigh_slot(i)
        arrive(c_slot, None, last)
        stat_slot(last).wait_recv()
        value_slot(last)
        weigh_slot(last)
    else:
        for i in (TWIN, NEAR):
            c_slot(i).wait_recv()
            value_slot(i)
            stat_slot(i).wait_recv()
            weigh_slot(i)

        def back_step(d):
            arrive(c_slot, None, d)
            value_slot(d)
            stat_slot(d).wait_recv()
            weigh_slot(d)

        each(back_step)

    dk_low = [dk[a].astype(BF16) for a in range(groups)]
    dv_low = [dv[a].astype(BF16) for a in range(groups)]

    def share(k, which):
        at = half_at(which)
        total = part_out[k]
        for a in range(groups):
            total = total + mm_nt(dk_low[a], w_k[a, at, :]) + mm_nt(dv_low[a], w_v[a, at, :])
        return total.astype(BF16)

    give[...] = share(0, 1 - h)
    swap = copy(give, take, h_send, h_recv, twin)
    swap.start()
    mine = mm(pick, share(1, h))
    pick_twin = picked(1 - h)
    swap.wait_recv()
    out[...] = (mine + mm(pick_twin, take[...])).astype(BF16)

    swap.wait_send()
    for i in (NEAR, TWIN):
        for copy_of in (x_slot, c_slot, stat_slot):
            copy_of(i).wait_send()
    for w_copy in w_copies:
        w_copy.wait_send()
    each(lambda d: stat_slot(d).wait_send())
    each_direct(lambda d: x_slot(d).wait_send())
    each_direct(lambda d: c_slot(d).wait_send())
    if line:
        @pl.when(inner)
        def _():
            x_hop().wait_send()
            c_hop().wait_send()


def body(features, cotangent, w_query, w_key, w_value, w_out, adjacency, partner, node_order):
    n, nb = lax.axis_size("slab"), lax.axis_size("blk")
    rows, width = features.shape
    cols = w_query.shape[1]
    half, block = width // 2, rows // 2
    lanes = (cols // HEAD_DIM) * block
    far = n + 1
    keys = (n + 2) * block
    kept = far if n == 4 and nb == 2 else 1
    vm, dma = pltpu.VMEM, pltpu.SemaphoreType.DMA
    vmem, hbm = (pl.BlockSpec(memory_space=m) for m in (pltpu.VMEM, pltpu.HBM))
    return pl.pallas_call(
        functools.partial(kernel, n, nb),
        out_shape=jax.ShapeDtypeStruct((rows, half), BF16),
        in_specs=[hbm] * 9,
        out_specs=vmem,
        scratch_shapes=[
            vm((rows, width), BF16), vm((rows, width), BF16),
            vm((2, width, cols), BF16), vm((2, width, cols), BF16), vm((2, width, cols), BF16),
            vm((2, cols, width), BF16), pltpu.SMEM(adjacency.shape, jnp.int32),
            pltpu.SMEM(adjacency.shape, jnp.int32), vm((1, rows), jnp.int32), dma((9,)),
            vm((block, width), BF16), vm((block, width), BF16),
            vm((far, block, width), BF16), vm((far, block, width), BF16),
            vm((2, block, cols), BF16), vm((2, block, cols), BF16), vm((2, cols, keys), BF16),
            vm((2, lanes, cols), BF16), vm((2, lanes, cols), BF16),
            vm((far, 2, lanes, cols), BF16), vm((kept, 2, lanes, cols), BF16),
            vm((kept, 2, block, lanes), F32),
            vm((2, block, lanes), F32), vm((2, block, lanes), F32),
            vm((far, 2, block, lanes), F32), vm((far, 2, block, lanes), F32),
            vm((far, 2, block, lanes), F32), vm((2, keys, lanes), BF16),
            vm((2, 8, lanes), F32), vm((far, 2, 8, lanes), F32),
            vm((2, 8, 128), F32), vm((2, 8, 128), F32), vm((2, 8, 128), F32), vm((far, 2, 8, 128), F32),
            vm((2, block, cols), F32), vm((2, block, cols), F32), vm((2, block, half), F32),
            vm((block, half), BF16), vm((block, half), BF16),
        ] + [dma((far,)) for _ in range(6)]
        + [dma((4,)), dma((4,)), dma(()), dma(()), dma((2,)), pltpu.SemaphoreType.REGULAR((far,))],
        compiler_params=pltpu.CompilerParams(
            collective_id=0, has_side_effects=True, vmem_limit_bytes=(40 if n <= 4 else 63) * 1024 * 1024
        ),
    )(*(
        pltpu.with_memory_space_constraint(v, pltpu.HBM) for v in (
            features, cotangent, w_query, w_key, w_value, w_out,
            adjacency, partner.T, node_order.reshape(1, rows),
        )
    ))


def solution(mesh):
    rows = P(("parts", "slab", "blk"), None)
    in_specs = (
        rows, rows,
        P(None, "head"), P(None, "head"), P(None, "head"), P("head", None),
        rows, P(None, ("parts", "slab", "blk")), P(("parts", "slab", "blk")),
    )
    return jax.shard_map(
        body, mesh=mesh, in_specs=in_specs,
        out_specs=P(("parts", "slab", "blk"), "head"), check_vma=False,
    )
```

```python
import functools

import jax
import jax.numpy as jnp
from jax import lax
from jax.experimental import pallas as pl
from jax.experimental.pallas import tpu as pltpu
from jax.sharding import PartitionSpec as P

HEAD_DIM = 64
OFF = -1e30
NT = (((1,), (1,)), ((), ()))
TN = (((0,), (0,)), ((), ()))
F32, BF16 = jnp.float32, jnp.bfloat16
MESH = pl.DeviceIdType.MESH


def mm(a, b):
    return jnp.dot(a, b, preferred_element_type=F32)


def mm_nt(a, b):
    return lax.dot_general(a, b, NT, preferred_element_type=F32)


def kernel(
    n, nb,
    feat_hbm, cot_hbm, w_q_hbm, w_k_hbm, w_v_hbm, w_o_hbm, adj_hbm, part_hbm, order_hbm, out,
    feat, cot, w_q, w_k, w_v, w_o, adj, part, order, fetch,
    own_x, own_c, rx, rc, k_own, v_own, kt_all, qm_own, gm_own,
    qm_far, gm_far, gp_far, e_own, g_own, e_far, g_far, s_back, ds_all, rows_own, rows_far,
    stat, stat_near, stat_twin, stat_far,
    dk, dv, part_out, give, take,
    x_send, x_recv, c_send, c_recv, t_send, t_recv, w_send, w_recv, h_send, h_recv, hop_send, acks,
):
    rows, width = feat.shape
    half = width // 2
    cols = w_q.shape[2]
    groups = 2
    heads = cols // HEAD_DIM
    block = rows // 2
    lanes = heads * block
    scale = HEAD_DIM ** -0.5
    NEAR, TWIN = 0, n
    h, slab, x = (lax.axis_index(a) for a in ("head", "slab", "blk"))
    twin = {"head": 1 - h}
    near = {"blk": lax.rem(x + jnp.where(h == 0, nb - 1, 1), nb), "head": 1 - h}

    def onward(d):
        return {"slab": lax.rem(slab + d, n)}

    line = n == 4 and nb == 2
    at_start, at_end = slab == 0, slab == n - 1
    inner = jnp.logical_and(slab > 0, slab < n - 1)

    def each(f):
        if n <= 4:
            for d in range(1, n):
                f(d)
        else:
            lax.fori_loop(1, n, lambda d, c: (f(d), c)[1], 0)

    def slots(f):
        f(TWIN)
        f(NEAR)
        each(f)

    def each_direct(f):
        if line:
            f(2)
            pl.when(jnp.logical_not(at_end))(lambda: f(1))
            pl.when(jnp.logical_not(at_start))(lambda: f(3))
        else:
            each(f)

    weights = (w_q, w_k, w_v, w_o)
    loads = [
        pltpu.make_async_copy(src, dst, fetch.at[i])
        for i, (src, dst) in enumerate((
            (order_hbm, order), (feat_hbm, feat), (cot_hbm, cot), (w_q_hbm, w_q.at[h]),
            (w_k_hbm, w_k.at[h]), (w_v_hbm, w_v.at[h]), (w_o_hbm, w_o.at[h]),
            (adj_hbm, adj), (part_hbm, part),
        ))
    ]
    for load in loads:
        load.start()
    barrier = pltpu.get_barrier_semaphore()

    def greet(where):
        pl.semaphore_signal(barrier, inc=1, device_id=where, device_id_type=MESH)

    def ack(where, k):
        pl.semaphore_signal(acks.at[k], inc=1, device_id=where, device_id_type=MESH)

    def answered(k):
        pl.semaphore_wait(acks.at[k], 1)

    if line:
        pl.when(h == 0)(lambda: greet(twin))
        pl.when(x == 0)(lambda: greet(near))
        for d in range(1, n):
            pl.when(slab + d < n)(lambda d=d: greet({"slab": slab + d}))
    else:
        greet(near)
        greet(twin)
        each(lambda d: greet(onward(d)))

    def enter():
        if line:
            earlier = slab + x + h
            pl.when(earlier > 0)(lambda: pl.semaphore_wait(barrier, earlier))
            for d in range(1, n):
                pl.when(slab >= d)(lambda d=d: ack({"slab": slab - d}, d))
            pl.when(x == 1)(lambda: ack(near, NEAR))
            pl.when(h == 1)(lambda: ack(twin, TWIN))
        else:
            pl.semaphore_wait(barrier, n + 1)

    def copy(src, dst, send, recv, where):
        return pltpu.make_async_remote_copy(
            src_ref=src, dst_ref=dst, send_sem=send, recv_sem=recv,
            device_id=where, device_id_type=MESH,
        )

    def slot_copy(own, far, send, recv, i):
        where = near if isinstance(i, int) and i == NEAR else twin if isinstance(i, int) and i == TWIN else onward(i)
        return copy(own, far.at[i], send.at[i], recv.at[i], where)

    x_slot = functools.partial(slot_copy, own_x, rx, x_send, x_recv)
    c_slot = functools.partial(slot_copy, own_c, rc, c_send, c_recv)

    def stat_slot(i):
        own = stat
        if isinstance(i, int) and i in (NEAR, TWIN):
            own = stat_near if i == NEAR else stat_twin
        return slot_copy(own, stat_far, t_send, t_recv, i)

    def hop_copy(far, recv, k):
        up = slab == n - 2
        slot = jnp.where(up, 3, 1)
        return copy(
            far.at[2], far.at[slot], hop_send.at[k], recv.at[slot],
            {"slab": jnp.where(up, n - 1, 0)},
        )

    x_hop = functools.partial(hop_copy, rx, x_recv, 0)
    c_hop = functools.partial(hop_copy, rc, c_recv, 1)

    w_copies = [
        copy(w.at[h], w.at[h], w_send.at[i], w_recv.at[i], twin) for i, w in enumerate(weights)
    ]

    def send_slab(copy_of, plan, wait=False):
        for z, ds in plan.items():
            @pl.when(slab == z)
            def _(z=z, ds=ds):
                for d in ds:
                    if wait and z + d < n:
                        answered(d)
                    copy_of(d).start()

    loads[0].wait()
    loads[1].wait()

    def picked(b):
        places = order[:, pl.ds(pl.multiple_of(b * block, block), block)]
        hot = lax.broadcasted_iota(jnp.int32, (rows, block), 0) == places
        return jnp.where(hot, 1.0, 0.0).astype(BF16)

    pick = picked(h)
    own_x[...] = lax.dot_general(pick, feat[...], TN, preferred_element_type=F32).astype(BF16)

    enter()
    if line:
        send_slab(x_slot, {0: (1, 2), 1: (3, 1), 2: (2, 1, 3), 3: (2, 3)}, wait=True)
        pl.when(x == 0)(lambda: answered(NEAR))
        pl.when(h == 0)(lambda: answered(TWIN))
    else:
        each_direct(lambda d: x_slot(d).start())
    x_slot(NEAR).start()
    x_slot(TWIN).start()
    if line:
        send_slab(x_slot, {1: (2,)}, wait=True)

    loads[2].wait()
    own_c[...] = lax.dot_general(pick, cot[...], TN, preferred_element_type=F32).astype(BF16)
    if line:
        send_slab(c_slot, {0: (1, 2), 1: (3,), 2: (2, 1), 3: (3, 2)})
    else:
        each_direct(lambda d: c_slot(d).start())
    c_slot(NEAR).start()
    c_slot(TWIN).start()

    for i in range(4):
        loads[3 + i].wait()
        w_copies[i].start()
    for load in loads[7:]:
        load.wait()

    lane_head = lax.broadcasted_iota(jnp.int32, (1, cols), 1) // HEAD_DIM
    masks = [jnp.where(lane_head == i, 1.0, 0.0).astype(BF16) for i in range(heads)]

    def masked(value):
        return jnp.concatenate([value * mask for mask in masks], axis=0)

    def weight_flag(flag):
        return jnp.where(flag > 0, 1.0, 0.0).astype(F32)

    def flag_of(i):
        return weight_flag(adj[h, 2 * h] if i == NEAR else adj[h, 2 - 2 * h])

    def far_weight(i):
        if isinstance(i, int) and i in (NEAR, TWIN):
            return flag_of(i)
        source = lax.rem(slab + n - i, n)
        total = jnp.float32(0.0)
        for m in range(3):
            total = total + jnp.where(lax.div(part[h, m], 2 * nb) == source, 1.0, 0.0)
        return total

    def bias(w):
        return jnp.where(w > 0.0, 0.0, OFF).astype(F32)

    def key_cols(i):
        if isinstance(i, int):
            return pl.ds(i * block, block)
        return pl.ds(pl.multiple_of(i * block, block), block)

    for w_copy in w_copies:
        w_copy.wait_recv()

    xs, cs = own_x[...], own_c[...]
    for a in range(groups):
        q = (mm(xs, w_q[a]).astype(BF16) * scale).astype(BF16)
        k32 = mm(xs, w_k[a])
        k = k32.astype(BF16)
        v = mm(xs, w_v[a]).astype(BF16)
        qm, gm = masked(q), masked(mm_nt(cs, w_o[a]).astype(BF16))
        k_own[a] = k
        v_own[a] = v
        kt_all[a, :, key_cols(n + 1)] = k32.T.astype(BF16)
        qm_own[a] = qm
        gm_own[a] = gm
        s = mm_nt(k, qm)
        g = mm_nt(v, gm)
        top = jnp.max(s, axis=0, keepdims=True)
        e = jnp.exp(s - top)
        e_own[a] = e
        g_own[a] = g
        rows_own[a, 0:1] = top
        rows_own[a, 1:2] = jnp.sum(e, axis=0, keepdims=True)
        rows_own[a, 2:3] = jnp.sum(e * g, axis=0, keepdims=True)

    def forward_slot(i):
        xi = rx[i]
        for a in range(groups):
            q = (mm(xi, w_q[a]).astype(BF16) * scale).astype(BF16)
            k32 = mm(xi, w_k[a])
            v = mm(xi, w_v[a]).astype(BF16)
            kt_all[a, :, key_cols(i)] = k32.T.astype(BF16)
            qm = masked(q)
            qm_far[i, a] = qm
            s = mm_nt(k32.astype(BF16), qm_own[a])
            g = mm_nt(v, gm_own[a])
            top = jnp.max(s, axis=0, keepdims=True)
            e = jnp.exp(s - top)
            e_far[i, a] = e
            g_far[i, a] = g
            rows_far[i, a, 0:1] = top
            rows_far[i, a, 1:2] = jnp.sum(e, axis=0, keepdims=True)
            rows_far[i, a, 2:3] = jnp.sum(e * g, axis=0, keepdims=True)
            s_back[i, a] = mm_nt(k_own[a], qm)

    def kept(i):
        return i if line else 0

    def value_slot(i):
        ci = rc[i]
        for a in range(groups):
            gm = masked(mm_nt(ci, w_o[a]).astype(BF16))
            gm_far[kept(i), a] = gm
            gp_far[kept(i), a] = mm_nt(v_own[a], gm)

    first, last = (jnp.where(at_start, 3, 1), jnp.where(at_start, 1, 3)) if line else (None, None)

    def arrive(copy_of, hop, i):
        copy_of(i).wait_recv()
        if hop is not None:
            @pl.when(inner)
            def _():
                hop().start()

    x_slot(TWIN).wait_recv()
    forward_slot(TWIN)
    x_slot(NEAR).wait_recv()
    forward_slot(NEAR)
    if line:
        arrive(x_slot, None, first)
        forward_slot(first)
        c_slot(TWIN).wait_recv()
        value_slot(TWIN)
        arrive(x_slot, x_hop, 2)
        send_slab(c_slot, {1: (1, 2), 2: (3,)})
        forward_slot(2)
        c_slot(NEAR).wait_recv()
        value_slot(NEAR)
        arrive(x_slot, None, last)
        forward_slot(last)
    else:
        def step(d):
            arrive(x_slot, None, d)
            forward_slot(d)

        each(step)

    tiles = lanes // 128

    def pack(ref, at, top, dot):
        for j in range(tiles):
            part_cols = slice(j * 128, (j + 1) * 128)
            ref[at, j:j + 1, :] = top[:, part_cols]
            ref[at, tiles + j:tiles + j + 1, :] = dot[:, part_cols]

    def unpack(tile):
        return (
            jnp.concatenate([tile[j:j + 1, :] for j in range(tiles)], axis=1),
            jnp.concatenate([tile[tiles + j:tiles + j + 1, :] for j in range(tiles)], axis=1),
        )

    for a in range(groups):
        rows_own[a, 3:4] = rows_own[a, 0:1]

        def far_top(i):
            rows_own[a, 3:4] = jnp.maximum(
                rows_own[a, 3:4], rows_far[i, a, 0:1] + bias(far_weight(i))
            )

        slots(far_top)
        top = rows_own[a, 3:4]
        share_own = jnp.exp(rows_own[a, 0:1] - top)
        rows_own[a, 4:5] = rows_own[a, 1:2] * share_own
        rows_own[a, 5:6] = rows_own[a, 2:3] * share_own

        def far_sum(i):
            w = far_weight(i)
            f = w * jnp.exp(rows_far[i, a, 0:1] + (bias(w) - top))
            rows_far[i, a, 3:4] = f
            rows_own[a, 4:5] += f * rows_far[i, a, 1:2]
            rows_own[a, 5:6] += f * rows_far[i, a, 2:3]

        slots(far_sum)
        inverse = 1.0 / rows_own[a, 4:5]
        dot = rows_own[a, 5:6] * inverse
        row_total = top + jnp.log(rows_own[a, 4:5])
        rows_own[a, 3:4] = share_own * inverse
        rows_own[a, 4:5] = inverse
        rows_own[a, 5:6] = dot
        pack(stat, a, row_total, dot)
        pack(stat_near, a, jnp.where(flag_of(NEAR) > 0.0, row_total, -OFF), dot)
        pack(stat_twin, a, jnp.where(flag_of(TWIN) > 0.0, row_total, -OFF), dot)

    if line:
        pl.when(at_start)(lambda: answered(3))
    stat_slot(TWIN).start()
    stat_slot(NEAR).start()
    each(lambda d: stat_slot(d).start())

    if line:
        arrive(c_slot, None, first)
        arrive(c_slot, c_hop, 2)

    def half_at(which):
        return pl.ds(pl.multiple_of(which * half, half), half)

    for a in range(groups):
        p = e_own[a] * rows_own[a, 3:4]
        ds = (p * (g_own[a] - rows_own[a, 5:6])).astype(BF16)
        ds_all[a, key_cols(n + 1)] = ds
        dv[a] = mm(p.astype(BF16), gm_own[a])
        dk[a] = mm(ds, qm_own[a])

        def query_grad(i):
            f = rows_far[i, a, 3:4] * rows_own[a, 4:5]
            ds_all[a, key_cols(i)] = (
                e_far[i, a] * f * (g_far[i, a] - rows_own[a, 5:6])
            ).astype(BF16)

        slots(query_grad)
        dq = jnp.concatenate([
            mm(kt_all[a, j * HEAD_DIM:(j + 1) * HEAD_DIM, :], ds_all[a, :, j * block:(j + 1) * block])
            for j in range(heads)
        ], axis=0)
        dq_low = (dq.T * scale).astype(BF16)
        for k, which in enumerate((1 - h, h)):
            piece = mm_nt(dq_low, w_q[a, half_at(which), :])
            if a == 0:
                part_out[k] = piece
            else:
                part_out[k] += piece

    def weigh_slot(i):
        for a in range(groups):
            row_total, dot = unpack(stat_far[i, a])
            if isinstance(i, int) and i in (NEAR, TWIN):
                p = jnp.exp(s_back[i, a] - row_total)
            else:
                w = far_weight(i)
                p = jnp.exp(s_back[i, a] - jnp.where(w > 0.0, row_total, -OFF)) * w
            ds = (p * (gp_far[kept(i), a] - dot)).astype(BF16)
            dv[a] += mm(p.astype(BF16), gm_far[kept(i), a])
            dk[a] += mm(ds, qm_far[i, a])

    if line:
        value_slot(first)
        value_slot(2)
        for i in (TWIN, NEAR, first, 2):
            stat_slot(i).wait_recv()
        for i in (TWIN, NEAR, first, 2):
            weigh_slot(i)
        arrive(c_slot, None, last)
        stat_slot(last).wait_recv()
        value_slot(last)
        weigh_slot(last)
    else:
        for i in (TWIN, NEAR):
            c_slot(i).wait_recv()
            value_slot(i)
            stat_slot(i).wait_recv()
            weigh_slot(i)

        def back_step(d):
            arrive(c_slot, None, d)
            value_slot(d)
            stat_slot(d).wait_recv()
            weigh_slot(d)

        each(back_step)

    dk_low = [dk[a].astype(BF16) for a in range(groups)]
    dv_low = [dv[a].astype(BF16) for a in range(groups)]

    def share(k, which):
        at = half_at(which)
        total = part_out[k]
        for a in range(groups):
            total = total + mm_nt(dk_low[a], w_k[a, at, :]) + mm_nt(dv_low[a], w_v[a, at, :])
        return total.astype(BF16)

    give[...] = share(0, 1 - h)
    swap = copy(give, take, h_send, h_recv, twin)
    swap.start()
    mine = mm(pick, share(1, h))
    pick_twin = picked(1 - h)
    swap.wait_recv()
    out[...] = (mine + mm(pick_twin, take[...])).astype(BF16)

    swap.wait_send()
    for i in (NEAR, TWIN):
        for copy_of in (x_slot, c_slot, stat_slot):
            copy_of(i).wait_send()
    for w_copy in w_copies:
        w_copy.wait_send()
    each(lambda d: stat_slot(d).wait_send())
    each_direct(lambda d: x_slot(d).wait_send())
    each_direct(lambda d: c_slot(d).wait_send())
    if line:
        @pl.when(inner)
        def _():
            x_hop().wait_send()
            c_hop().wait_send()


def body(features, cotangent, w_query, w_key, w_value, w_out, adjacency, partner, node_order):
    n, nb = lax.axis_size("slab"), lax.axis_size("blk")
    rows, width = features.shape
    cols = w_query.shape[1]
    half, block = width // 2, rows // 2
    lanes = (cols // HEAD_DIM) * block
    far = n + 1
    keys = (n + 2) * block
    kept = far if n == 4 and nb == 2 else 1
    vm, dma = pltpu.VMEM, pltpu.SemaphoreType.DMA
    vmem, hbm = (pl.BlockSpec(memory_space=m) for m in (pltpu.VMEM, pltpu.HBM))
    return pl.pallas_call(
        functools.partial(kernel, n, nb),
        out_shape=jax.ShapeDtypeStruct((rows, half), BF16),
        in_specs=[hbm] * 9,
        out_specs=vmem,
        scratch_shapes=[
            vm((rows, width), BF16), vm((rows, width), BF16),
            vm((2, width, cols), BF16), vm((2, width, cols), BF16), vm((2, width, cols), BF16),
            vm((2, cols, width), BF16), pltpu.SMEM(adjacency.shape, jnp.int32),
            pltpu.SMEM(adjacency.shape, jnp.int32), vm((1, rows), jnp.int32), dma((9,)),
            vm((block, width), BF16), vm((block, width), BF16),
            vm((far, block, width), BF16), vm((far, block, width), BF16),
            vm((2, block, cols), BF16), vm((2, block, cols), BF16), vm((2, cols, keys), BF16),
            vm((2, lanes, cols), BF16), vm((2, lanes, cols), BF16),
            vm((far, 2, lanes, cols), BF16), vm((kept, 2, lanes, cols), BF16),
            vm((kept, 2, block, lanes), F32),
            vm((2, block, lanes), F32), vm((2, block, lanes), F32),
            vm((far, 2, block, lanes), F32), vm((far, 2, block, lanes), F32),
            vm((far, 2, block, lanes), F32), vm((2, keys, lanes), BF16),
            vm((2, 8, lanes), F32), vm((far, 2, 8, lanes), F32),
            vm((2, 8, 128), F32), vm((2, 8, 128), F32), vm((2, 8, 128), F32), vm((far, 2, 8, 128), F32),
            vm((2, block, cols), F32), vm((2, block, cols), F32), vm((2, block, half), F32),
            vm((block, half), BF16), vm((block, half), BF16),
        ] + [dma((far,)) for _ in range(6)]
        + [dma((4,)), dma((4,)), dma(()), dma(()), dma((2,)), pltpu.SemaphoreType.REGULAR((far,))],
        compiler_params=pltpu.CompilerParams(
            collective_id=0, has_side_effects=True, vmem_limit_bytes=(40 if n <= 4 else 63) * 1024 * 1024
        ),
    )(*(
        pltpu.with_memory_space_constraint(v, pltpu.HBM) for v in (
            features, cotangent, w_query, w_key, w_value, w_out,
            adjacency, partner.T, node_order.reshape(1, rows),
        )
    ))


def solution(mesh):
    rows = P(("parts", "slab", "blk"), None)
    in_specs = (
        rows, rows,
        P(None, "head"), P(None, "head"), P(None, "head"), P("head", None),
        rows, P(None, ("parts", "slab", "blk")), P(("parts", "slab", "blk")),
    )
    return jax.shard_map(
        body, mesh=mesh, in_specs=in_specs,
        out_specs=P(("parts", "slab", "blk"), "head"), check_vma=False,
    )
```

```python
import functools

import jax
import jax.numpy as jnp
from jax import lax
from jax.experimental import pallas as pl
from jax.experimental.pallas import tpu as pltpu
from jax.sharding import PartitionSpec as P

HEAD_DIM = 64
OFF = -1e30
NT = (((1,), (1,)), ((), ()))
TN = (((0,), (0,)), ((), ()))
F32, BF16 = jnp.float32, jnp.bfloat16
MESH = pl.DeviceIdType.MESH


def mm(a, b):
    return jnp.dot(a, b, preferred_element_type=F32)


def mm_nt(a, b):
    return lax.dot_general(a, b, NT, preferred_element_type=F32)


def kernel(
    n, nb,
    feat_hbm, cot_hbm, w_q_hbm, w_k_hbm, w_v_hbm, w_o_hbm, adj_hbm, part_hbm, order_hbm, out,
    feat, cot, w_q, w_k, w_v, w_o, adj, part, order, fetch,
    own_x, own_c, rx, rc, k_own, v_own, kt_all, qm_own, gm_own,
    qm_far, gm_far, gp_far, e_own, g_own, e_far, g_far, s_back, ds_all, rows_own, rows_far,
    stat, stat_near, stat_twin, stat_far,
    dk, dv, part_out, give, take,
    x_send, x_recv, c_send, c_recv, t_send, t_recv, w_send, w_recv, h_send, h_recv, hop_send, acks,
):
    rows, width = feat.shape
    half = width // 2
    cols = w_q.shape[2]
    groups = 2
    heads = cols // HEAD_DIM
    block = rows // 2
    lanes = heads * block
    scale = HEAD_DIM ** -0.5
    NEAR, TWIN = 0, n
    h, slab, x = (lax.axis_index(a) for a in ("head", "slab", "blk"))
    twin = {"head": 1 - h}
    near = {"blk": lax.rem(x + jnp.where(h == 0, nb - 1, 1), nb), "head": 1 - h}

    def onward(d):
        return {"slab": lax.rem(slab + d, n)}

    line = n == 4 and nb == 2
    at_start, at_end = slab == 0, slab == n - 1
    inner = jnp.logical_and(slab > 0, slab < n - 1)
    outer = jnp.logical_not(inner)

    def each(f):
        if n <= 4:
            for d in range(1, n):
                f(d)
        else:
            lax.fori_loop(1, n, lambda d, c: (f(d), c)[1], 0)

    def slots(f):
        f(TWIN)
        f(NEAR)
        each(f)

    def each_direct(f):
        if line:
            f(2)
            pl.when(jnp.logical_not(at_end))(lambda: f(1))
            pl.when(jnp.logical_not(at_start))(lambda: f(3))
        else:
            each(f)

    weights = (w_q, w_k, w_v, w_o)
    loads = [
        pltpu.make_async_copy(src, dst, fetch.at[i])
        for i, (src, dst) in enumerate((
            (order_hbm, order), (feat_hbm, feat), (cot_hbm, cot), (w_q_hbm, w_q.at[h]),
            (w_k_hbm, w_k.at[h]), (w_v_hbm, w_v.at[h]), (w_o_hbm, w_o.at[h]),
            (adj_hbm, adj), (part_hbm, part),
        ))
    ]
    for load in loads:
        load.start()
    barrier = pltpu.get_barrier_semaphore()

    def greet(where):
        pl.semaphore_signal(barrier, inc=1, device_id=where, device_id_type=MESH)

    def ack(where, k):
        pl.semaphore_signal(acks.at[k], inc=1, device_id=where, device_id_type=MESH)

    def answered(k):
        pl.semaphore_wait(acks.at[k], 1)

    if line:
        pl.when(h == 0)(lambda: greet(twin))
        pl.when(x == 0)(lambda: greet(near))
        for d in range(1, n):
            pl.when(slab + d < n)(lambda d=d: greet({"slab": slab + d}))
    else:
        greet(near)
        greet(twin)
        each(lambda d: greet(onward(d)))

    def enter():
        if line:
            earlier = slab + x + h
            pl.when(earlier > 0)(lambda: pl.semaphore_wait(barrier, earlier))
            for d in range(1, n):
                pl.when(slab >= d)(lambda d=d: ack({"slab": slab - d}, d))
            pl.when(x == 1)(lambda: ack(near, NEAR))
            pl.when(h == 1)(lambda: ack(twin, TWIN))
        else:
            pl.semaphore_wait(barrier, n + 1)

    def copy(src, dst, send, recv, where):
        return pltpu.make_async_remote_copy(
            src_ref=src, dst_ref=dst, send_sem=send, recv_sem=recv,
            device_id=where, device_id_type=MESH,
        )

    def slot_copy(own, far, send, recv, i):
        where = near if isinstance(i, int) and i == NEAR else twin if isinstance(i, int) and i == TWIN else onward(i)
        return copy(own, far.at[i], send.at[i], recv.at[i], where)

    x_slot = functools.partial(slot_copy, own_x, rx, x_send, x_recv)
    c_slot = functools.partial(slot_copy, own_c, rc, c_send, c_recv)

    def stat_slot(i):
        own = stat
        if isinstance(i, int) and i in (NEAR, TWIN):
            own = stat_near if i == NEAR else stat_twin
        return slot_copy(own, stat_far, t_send, t_recv, i)

    def hop_copy(far, recv, k):
        up = slab == n - 2
        slot = jnp.where(up, 3, 1)
        return copy(
            far.at[2], far.at[slot], hop_send.at[k], recv.at[slot],
            {"slab": jnp.where(up, n - 1, 0)},
        )

    x_hop = functools.partial(hop_copy, rx, x_recv, 0)
    c_hop = functools.partial(hop_copy, rc, c_recv, 1)

    w_copies = [
        copy(w.at[h], w.at[h], w_send.at[i], w_recv.at[i], twin) for i, w in enumerate(weights)
    ]

    def send_slab(copy_of, plan, wait=False):
        for z, ds in plan.items():
            @pl.when(slab == z)
            def _(z=z, ds=ds):
                for d in ds:
                    if wait and z + d < n:
                        answered(d)
                    copy_of(d).start()

    loads[0].wait()
    loads[1].wait()

    def picked(b):
        places = order[:, pl.ds(pl.multiple_of(b * block, block), block)]
        hot = lax.broadcasted_iota(jnp.int32, (rows, block), 0) == places
        return jnp.where(hot, 1.0, 0.0).astype(BF16)

    pick = picked(h)
    own_x[...] = lax.dot_general(pick, feat[...], TN, preferred_element_type=F32).astype(BF16)

    enter()
    if line:
        send_slab(x_slot, {0: (1, 2), 1: (3, 1, 2), 2: (2, 1, 3), 3: (2, 3)}, wait=True)
        pl.when(x == 0)(lambda: answered(NEAR))
        pl.when(h == 0)(lambda: answered(TWIN))
    else:
        each_direct(lambda d: x_slot(d).start())
    x_slot(NEAR).start()
    x_slot(TWIN).start()

    loads[2].wait()
    own_c[...] = lax.dot_general(pick, cot[...], TN, preferred_element_type=F32).astype(BF16)
    if line:
        send_slab(c_slot, {0: (1, 2), 1: (3,), 2: (2, 1), 3: (3, 2)})
    else:
        each_direct(lambda d: c_slot(d).start())
    c_slot(NEAR).start()
    c_slot(TWIN).start()

    for i in range(4):
        loads[3 + i].wait()
        w_copies[i].start()
    for load in loads[7:]:
        load.wait()

    lane_head = lax.broadcasted_iota(jnp.int32, (1, cols), 1) // HEAD_DIM
    masks = [jnp.where(lane_head == i, 1.0, 0.0).astype(BF16) for i in range(heads)]

    def masked(value):
        return jnp.concatenate([value * mask for mask in masks], axis=0)

    def weight_flag(flag):
        return jnp.where(flag > 0, 1.0, 0.0).astype(F32)

    def flag_of(i):
        return weight_flag(adj[h, 2 * h] if i == NEAR else adj[h, 2 - 2 * h])

    def far_weight(i):
        if isinstance(i, int) and i in (NEAR, TWIN):
            return flag_of(i)
        source = lax.rem(slab + n - i, n)
        total = jnp.float32(0.0)
        for m in range(3):
            total = total + jnp.where(lax.div(part[h, m], 2 * nb) == source, 1.0, 0.0)
        return total

    def bias(w):
        return jnp.where(w > 0.0, 0.0, OFF).astype(F32)

    def key_cols(i):
        if isinstance(i, int):
            return pl.ds(i * block, block)
        return pl.ds(pl.multiple_of(i * block, block), block)

    for w_copy in w_copies:
        w_copy.wait_recv()

    xs, cs = own_x[...], own_c[...]
    for a in range(groups):
        q = (mm(xs, w_q[a]).astype(BF16) * scale).astype(BF16)
        k32 = mm(xs, w_k[a])
        k = k32.astype(BF16)
        v = mm(xs, w_v[a]).astype(BF16)
        qm, gm = masked(q), masked(mm_nt(cs, w_o[a]).astype(BF16))
        k_own[a] = k
        v_own[a] = v
        kt_all[a, :, key_cols(n + 1)] = k32.T.astype(BF16)
        qm_own[a] = qm
        gm_own[a] = gm
        s = mm_nt(k, qm)
        g = mm_nt(v, gm)
        top = jnp.max(s, axis=0, keepdims=True)
        e = jnp.exp(s - top)
        e_own[a] = e
        g_own[a] = g
        rows_own[a, 0:1] = top
        rows_own[a, 1:2] = jnp.sum(e, axis=0, keepdims=True)
        rows_own[a, 2:3] = jnp.sum(e * g, axis=0, keepdims=True)

    def forward_slot(i):
        xi = rx[i]
        for a in range(groups):
            q = (mm(xi, w_q[a]).astype(BF16) * scale).astype(BF16)
            k32 = mm(xi, w_k[a])
            v = mm(xi, w_v[a]).astype(BF16)
            kt_all[a, :, key_cols(i)] = k32.T.astype(BF16)
            qm = masked(q)
            qm_far[i, a] = qm
            s = mm_nt(k32.astype(BF16), qm_own[a])
            g = mm_nt(v, gm_own[a])
            top = jnp.max(s, axis=0, keepdims=True)
            e = jnp.exp(s - top)
            e_far[i, a] = e
            g_far[i, a] = g
            rows_far[i, a, 0:1] = top
            rows_far[i, a, 1:2] = jnp.sum(e, axis=0, keepdims=True)
            rows_far[i, a, 2:3] = jnp.sum(e * g, axis=0, keepdims=True)
            s_back[i, a] = mm_nt(k_own[a], qm)

    def kept(i):
        return i if line else 0

    def value_slot(i):
        ci = rc[i]
        for a in range(groups):
            gm = masked(mm_nt(ci, w_o[a]).astype(BF16))
            gm_far[kept(i), a] = gm
            gp_far[kept(i), a] = mm_nt(v_own[a], gm)

    first, last = (jnp.where(at_start, 3, 1), jnp.where(at_start, 1, 3)) if line else (None, None)

    def arrive(copy_of, hop, i):
        copy_of(i).wait_recv()
        if hop is not None:
            @pl.when(inner)
            def _():
                hop().start()

    x_slot(TWIN).wait_recv()
    forward_slot(TWIN)
    x_slot(NEAR).wait_recv()
    forward_slot(NEAR)
    if line:
        arrive(x_slot, None, first)
        forward_slot(first)
        c_slot(TWIN).wait_recv()
        value_slot(TWIN)
        arrive(x_slot, x_hop, 2)
        send_slab(c_slot, {1: (1, 2), 2: (3,)})
        forward_slot(2)
        c_slot(NEAR).wait_recv()
        value_slot(NEAR)
        arrive(x_slot, None, last)
        forward_slot(last)
    else:
        def step(d):
            arrive(x_slot, None, d)
            forward_slot(d)

        each(step)

    tiles = lanes // 128

    def pack(ref, at, top, dot):
        for j in range(tiles):
            part_cols = slice(j * 128, (j + 1) * 128)
            ref[at, j:j + 1, :] = top[:, part_cols]
            ref[at, tiles + j:tiles + j + 1, :] = dot[:, part_cols]

    def unpack(tile):
        return (
            jnp.concatenate([tile[j:j + 1, :] for j in range(tiles)], axis=1),
            jnp.concatenate([tile[tiles + j:tiles + j + 1, :] for j in range(tiles)], axis=1),
        )

    for a in range(groups):
        rows_own[a, 3:4] = rows_own[a, 0:1]

        def far_top(i):
            rows_own[a, 3:4] = jnp.maximum(
                rows_own[a, 3:4], rows_far[i, a, 0:1] + bias(far_weight(i))
            )

        slots(far_top)
        top = rows_own[a, 3:4]
        share_own = jnp.exp(rows_own[a, 0:1] - top)
        rows_own[a, 4:5] = rows_own[a, 1:2] * share_own
        rows_own[a, 5:6] = rows_own[a, 2:3] * share_own

        def far_sum(i):
            w = far_weight(i)
            f = w * jnp.exp(rows_far[i, a, 0:1] + (bias(w) - top))
            rows_far[i, a, 3:4] = f
            rows_own[a, 4:5] += f * rows_far[i, a, 1:2]
            rows_own[a, 5:6] += f * rows_far[i, a, 2:3]

        slots(far_sum)
        inverse = 1.0 / rows_own[a, 4:5]
        dot = rows_own[a, 5:6] * inverse
        row_total = top + jnp.log(rows_own[a, 4:5])
        rows_own[a, 3:4] = share_own * inverse
        rows_own[a, 4:5] = inverse
        rows_own[a, 5:6] = dot
        pack(stat, a, row_total, dot)
        pack(stat_near, a, jnp.where(flag_of(NEAR) > 0.0, row_total, -OFF), dot)
        pack(stat_twin, a, jnp.where(flag_of(TWIN) > 0.0, row_total, -OFF), dot)

    if line:
        pl.when(at_start)(lambda: answered(3))
    each(lambda d: stat_slot(d).start())
    stat_slot(NEAR).start()
    stat_slot(TWIN).start()

    if line:
        arrive(c_slot, None, first)
        @pl.when(inner)
        def _():
            c_slot(2).wait_recv()
            c_hop().start()


    def half_at(which):
        return pl.ds(pl.multiple_of(which * half, half), half)

    for a in range(groups):
        p = e_own[a] * rows_own[a, 3:4]
        ds = (p * (g_own[a] - rows_own[a, 5:6])).astype(BF16)
        ds_all[a, key_cols(n + 1)] = ds
        dv[a] = mm(p.astype(BF16), gm_own[a])
        dk[a] = mm(ds, qm_own[a])

        def query_grad(i):
            f = rows_far[i, a, 3:4] * rows_own[a, 4:5]
            ds_all[a, key_cols(i)] = (
                e_far[i, a] * f * (g_far[i, a] - rows_own[a, 5:6])
            ).astype(BF16)

        slots(query_grad)
        dq = jnp.concatenate([
            mm(kt_all[a, j * HEAD_DIM:(j + 1) * HEAD_DIM, :], ds_all[a, :, j * block:(j + 1) * block])
            for j in range(heads)
        ], axis=0)
        dq_low = (dq.T * scale).astype(BF16)
        for k, which in enumerate((1 - h, h)):
            piece = mm_nt(dq_low, w_q[a, half_at(which), :])
            if a == 0:
                part_out[k] = piece
            else:
                part_out[k] += piece

    def weigh_slot(i):
        for a in range(groups):
            row_total, dot = unpack(stat_far[i, a])
            if isinstance(i, int) and i in (NEAR, TWIN):
                p = jnp.exp(s_back[i, a] - row_total)
            else:
                w = far_weight(i)
                p = jnp.exp(s_back[i, a] - jnp.where(w > 0.0, row_total, -OFF)) * w
            ds = (p * (gp_far[kept(i), a] - dot)).astype(BF16)
            dv[a] += mm(p.astype(BF16), gm_far[kept(i), a])
            dk[a] += mm(ds, qm_far[i, a])

    if line:
        value_slot(first)
        pl.when(outer)(lambda: c_slot(2).wait_recv())
        value_slot(2)
        for i in (TWIN, NEAR, first, 2):
            stat_slot(i).wait_recv()
        for i in (TWIN, NEAR, first, 2):
            weigh_slot(i)
        arrive(c_slot, None, last)
        stat_slot(last).wait_recv()
        value_slot(last)
        weigh_slot(last)
    else:
        for i in (TWIN, NEAR):
            c_slot(i).wait_recv()
            value_slot(i)
            stat_slot(i).wait_recv()
            weigh_slot(i)

        def back_step(d):
            arrive(c_slot, None, d)
            value_slot(d)
            stat_slot(d).wait_recv()
            weigh_slot(d)

        each(back_step)

    dk_low = [dk[a].astype(BF16) for a in range(groups)]
    dv_low = [dv[a].astype(BF16) for a in range(groups)]

    def share(k, which):
        at = half_at(which)
        total = part_out[k]
        for a in range(groups):
            total = total + mm_nt(dk_low[a], w_k[a, at, :]) + mm_nt(dv_low[a], w_v[a, at, :])
        return total.astype(BF16)

    give[...] = share(0, 1 - h)
    swap = copy(give, take, h_send, h_recv, twin)
    swap.start()
    mine = mm(pick, share(1, h))
    pick_twin = picked(1 - h)
    swap.wait_recv()
    out[...] = (mine + mm(pick_twin, take[...])).astype(BF16)

    swap.wait_send()
    for i in (NEAR, TWIN):
        for copy_of in (x_slot, c_slot, stat_slot):
            copy_of(i).wait_send()
    for w_copy in w_copies:
        w_copy.wait_send()
    each(lambda d: stat_slot(d).wait_send())
    each_direct(lambda d: x_slot(d).wait_send())
    each_direct(lambda d: c_slot(d).wait_send())
    if line:
        @pl.when(inner)
        def _():
            x_hop().wait_send()
            c_hop().wait_send()


def body(features, cotangent, w_query, w_key, w_value, w_out, adjacency, partner, node_order):
    n, nb = lax.axis_size("slab"), lax.axis_size("blk")
    rows, width = features.shape
    cols = w_query.shape[1]
    half, block = width // 2, rows // 2
    lanes = (cols // HEAD_DIM) * block
    far = n + 1
    keys = (n + 2) * block
    kept = far if n == 4 and nb == 2 else 1
    vm, dma = pltpu.VMEM, pltpu.SemaphoreType.DMA
    vmem, hbm = (pl.BlockSpec(memory_space=m) for m in (pltpu.VMEM, pltpu.HBM))
    return pl.pallas_call(
        functools.partial(kernel, n, nb),
        out_shape=jax.ShapeDtypeStruct((rows, half), BF16),
        in_specs=[hbm] * 9,
        out_specs=vmem,
        scratch_shapes=[
            vm((rows, width), BF16), vm((rows, width), BF16),
            vm((2, width, cols), BF16), vm((2, width, cols), BF16), vm((2, width, cols), BF16),
            vm((2, cols, width), BF16), pltpu.SMEM(adjacency.shape, jnp.int32),
            pltpu.SMEM(adjacency.shape, jnp.int32), vm((1, rows), jnp.int32), dma((9,)),
            vm((block, width), BF16), vm((block, width), BF16),
            vm((far, block, width), BF16), vm((far, block, width), BF16),
            vm((2, block, cols), BF16), vm((2, block, cols), BF16), vm((2, cols, keys), BF16),
            vm((2, lanes, cols), BF16), vm((2, lanes, cols), BF16),
            vm((far, 2, lanes, cols), BF16), vm((kept, 2, lanes, cols), BF16),
            vm((kept, 2, block, lanes), F32),
            vm((2, block, lanes), F32), vm((2, block, lanes), F32),
            vm((far, 2, block, lanes), F32), vm((far, 2, block, lanes), F32),
            vm((far, 2, block, lanes), F32), vm((2, keys, lanes), BF16),
            vm((2, 8, lanes), F32), vm((far, 2, 8, lanes), F32),
            vm((2, 8, 128), F32), vm((2, 8, 128), F32), vm((2, 8, 128), F32), vm((far, 2, 8, 128), F32),
            vm((2, block, cols), F32), vm((2, block, cols), F32), vm((2, block, half), F32),
            vm((block, half), BF16), vm((block, half), BF16),
        ] + [dma((far,)) for _ in range(6)]
        + [dma((4,)), dma((4,)), dma(()), dma(()), dma((2,)), pltpu.SemaphoreType.REGULAR((far,))],
        compiler_params=pltpu.CompilerParams(
            collective_id=0, has_side_effects=True, vmem_limit_bytes=(40 if n <= 4 else 63) * 1024 * 1024
        ),
    )(*(
        pltpu.with_memory_space_constraint(v, pltpu.HBM) for v in (
            features, cotangent, w_query, w_key, w_value, w_out,
            adjacency, partner.T, node_order.reshape(1, rows),
        )
    ))


def solution(mesh):
    rows = P(("parts", "slab", "blk"), None)
    in_specs = (
        rows, rows,
        P(None, "head"), P(None, "head"), P(None, "head"), P("head", None),
        rows, P(None, ("parts", "slab", "blk")), P(("parts", "slab", "blk")),
    )
    return jax.shard_map(
        body, mesh=mesh, in_specs=in_specs,
        out_specs=P(("parts", "slab", "blk"), "head"), check_vma=False,
    )
```
